256 devices in a mesh: blk: 8 (over x, y_hi), tile: 32 (over z, y_lo, core).
Axes of the slice: x: 4, y: 4 (y_hi: 2, y_lo: 2; y = y_hi * 2 + y_lo), z: 8, core: 2. Of those that a mesh axis runs over, the one named last changes fastest.
Arguments:
- grid_feat: bfloat16 [65536, 512], P(('blk', 'tile')), may hold values from -18 to 18
- queries: bfloat16 [65536, 512], P(('blk', 'tile')), may hold values from -90 to 90
- obs_keys: bfloat16 [2048, 512], P(('blk', 'tile')), may hold values from -4 to 4
- obs_values: bfloat16 [2048, 512], P(('blk', 'tile')), may hold values from -6 to 6
- block_mask: int32 [512, 16], P(('blk', 'tile')), may hold values from 0 to 1, as said below
- obs_valid: int32 [16], replicated, may hold values from 2 to 128, as said below
- out_weight: bfloat16 [512, 512], replicated, may hold values from -0.25 to 0.25
- conv_weight: bfloat16 [3, 3, 512, 512], replicated, may hold values from -0.09375 to 0.09375
Outputs:
- layer_out: bfloat16 [65536, 512], P(('blk', 'tile'))
The draws below stay inside these ranges and needn't reach their ends.
Inputs may be any that keep to these rules, and one draw needn't show every extreme that they name: `block_mask`: row t has a 1 in column t mod 16. `obs_valid`: at least one entry equals 128.
All inputs are finite; a program needn't handle non-finite values.
Results may differ from the reference program's by a relative error of at most 0.007.
Values may be sent and summed in bfloat16 or wider, within the bound.
A program may use at most 64 MiB of HBM per device.

```python
import jax
import jax.numpy as jnp
from jax import lax

D = 512
HEADS = 8
HEAD = 64
LON = 128
OBS_BLOCK = 128
TILES_DEV = 2
NTILES = 512
NQ = 65536
OBS = 2048
NOBLK = 16


def draw_obs_keys(key, part):
    own = jax.random.fold_in(key, 31)
    keys = jnp.clip(jax.random.normal(own, (OBS, D), jnp.float32), -4.0, 4.0)
    return keys.astype(jnp.bfloat16)


def draw_queries(key, part):
    own = jax.random.fold_in(key, 32)
    values = jnp.clip(jax.random.normal(own, (NQ, D), jnp.float32), -4.0, 4.0)
    return values.astype(jnp.bfloat16)


def draw_grid_feat(key, part):
    own = jax.random.fold_in(key, 33)
    values = jnp.clip(jax.random.normal(own, (NQ, D), jnp.float32), -5.0, 5.0)
    return values.astype(jnp.bfloat16)


def draw_block_mask(key, part):
    devices = NTILES // TILES_DEV
    level = jax.random.randint(jax.random.fold_in(key, 11), (devices,), 1, 9)
    tile_level = jnp.repeat(level, TILES_DEV)
    picks = jax.random.randint(jax.random.fold_in(key, 12), (NTILES, NOBLK), 0, 8)
    forced = jnp.arange(NTILES)[:, None] % NOBLK == jnp.arange(NOBLK)[None, :]
    return ((picks < tile_level[:, None]) | forced).astype(jnp.int32)


def draw_obs_valid(key, part):
    counts = jax.random.randint(jax.random.fold_in(key, 21), (NOBLK,), 2, OBS_BLOCK + 1)
    full = jax.random.randint(jax.random.fold_in(key, 22), (), 0, NOBLK)
    return jnp.where(jnp.arange(NOBLK) == full, OBS_BLOCK, counts).astype(jnp.int32)


def block_scale(stream_key, extent, shards, smallest, top_value):
    loudness, own = 1.0, jax.random.fold_in(stream_key, 6)
    for position, blocks in shards:
        draws = jnp.exp(jax.random.uniform(jax.random.fold_in(own, position), (blocks,), jnp.float32, smallest / len(shards), top_value / len(shards)))
        loudness = loudness * jnp.repeat(draws, extent[position] // blocks).reshape([-1 if axis == position else 1 for axis in range(len(extent))])
    return loudness


def scatter_about(own_key, dims, scale, reach, split=(), kind=jnp.bfloat16):
    entries = scale * jax.random.normal(own_key, dims, jnp.float32)
    if split:
        entries = entries * block_scale(own_key, dims, split, -0.22, 0.18)
    return jnp.clip(entries, -reach, reach).astype(kind)


def setup_inputs(seed: int = 0) -> dict:
    streams_of = jax.random.split(jax.random.key(seed), 9)
    grid_feat = draw_grid_feat(jax.random.fold_in(streams_of[8], 71), 0)
    queries = draw_queries(jax.random.fold_in(streams_of[8], 71), 0)
    obs_keys = draw_obs_keys(jax.random.fold_in(streams_of[8], 71), 0)
    obs_values = scatter_about(streams_of[3], (OBS, D), 1.0, 6.0, ((0, 256),))
    block_mask = draw_block_mask(jax.random.fold_in(streams_of[8], 71), 0)
    obs_valid = draw_obs_valid(jax.random.fold_in(streams_of[8], 71), 0)
    out_weight = scatter_about(streams_of[6], (D, D), D ** -0.5, 0.25)
    conv_weight = scatter_about(streams_of[7], (3, 3, D, D), (9 * D) ** -0.5, 0.09375)
    return dict(grid_feat=grid_feat, queries=queries, obs_keys=obs_keys, obs_values=obs_values, block_mask=block_mask, obs_valid=obs_valid, out_weight=out_weight, conv_weight=conv_weight)


def reference(grid_feat, queries, obs_keys, obs_values, block_mask, obs_valid, out_weight, conv_weight):
    rows = jnp.arange(OBS, dtype=jnp.int32)
    key_block = rows // OBS_BLOCK
    onehot = (key_block[:, None] == jnp.arange(NOBLK, dtype=jnp.int32)[None, :]).astype(jnp.float32)
    limits = lax.optimization_barrier(jnp.sum(jnp.where(onehot > 0.5, obs_valid[None, :], 0), axis=1))
    key_ok = rows % OBS_BLOCK < limits
    keys = obs_keys.astype(jnp.float32).reshape(OBS, HEADS, HEAD)
    values = obs_values.astype(jnp.float32).reshape(OBS, HEADS, HEAD)
    scale = HEAD ** (-0.5)
    blocks = NTILES // TILES_DEV
    query_blocks = queries.reshape(blocks, TILES_DEV, LON, HEADS, HEAD)
    mask_blocks = block_mask.reshape(blocks, TILES_DEV, NOBLK)

    def one_block(pair):
        query_rows, mask_rows = pair
        wanted = jnp.dot(mask_rows.astype(jnp.float32), onehot.T, precision=lax.Precision.HIGHEST) > 0.5
        allowed = wanted & key_ok[None, :]
        scores = jnp.einsum('tqhd,khd->htqk', query_rows.astype(jnp.float32), keys) * scale
        scores = jnp.where(allowed[None, :, None, :], scores, -jnp.inf)
        top = lax.optimization_barrier(jnp.max(scores, axis=-1, keepdims=True))
        weights = jnp.exp(scores - top)
        total = lax.optimization_barrier(jnp.sum(weights, axis=-1))
        rounded = lax.optimization_barrier(weights.astype(jnp.bfloat16)).astype(jnp.float32)
        mixed = jnp.einsum('htqk,khd->htqd', rounded, values) / total[..., None]
        return jnp.transpose(mixed, (1, 2, 0, 3)).reshape(TILES_DEV * LON, D).astype(jnp.bfloat16)
    mixed = lax.map(one_block, (query_blocks, mask_blocks)).reshape(NQ, D)
    projected = jnp.dot(mixed, out_weight, preferred_element_type=jnp.float32)
    hidden = lax.optimization_barrier((grid_feat.astype(jnp.float32) + projected).astype(jnp.bfloat16))
    wide = hidden.astype(jnp.float32)
    normed = (wide * lax.rsqrt(lax.optimization_barrier(jnp.mean(wide * wide, axis=-1, keepdims=True)) + 1e-06)).astype(jnp.bfloat16)
    field = normed.reshape(NTILES, LON, D)
    padded = jnp.pad(field, ((1, 1), (0, 0), (0, 0)))
    summed = jnp.zeros((NQ, D), jnp.float32)
    for lat_off in range(3):
        for lon_off in range(3):
            moved = jnp.roll(padded[lat_off:lat_off + NTILES], 1 - lon_off, axis=1)
            summed = summed + jnp.dot(moved.reshape(NQ, D), conv_weight[lat_off, lon_off], preferred_element_type=jnp.float32)
    return (wide + summed).astype(jnp.bfloat16)
```

```python
import jax
import jax.numpy as jnp
from jax import lax
from jax.experimental import pallas as pl
from jax.experimental.pallas import tpu as pltpu
from jax.sharding import PartitionSpec as P

MESH = pl.DeviceIdType.MESH
NX, NY, NZ = 4, 4, 8
LON = 128
D = 512
ROWS = 256
PAIRS = 4
NEG = -1e30
F32 = jnp.float32
BF16 = jnp.bfloat16


def ring(i, n):
    return lax.rem(i + n, n)


def device(x, y, z, core):
    return (x * 2 + y // 2, z * 4 + lax.rem(y, 2) * 2 + core)


def kernel(
    mask_ref, valid_ref, feat_hbm, q_hbm, k_hbm, v_hbm, wo_hbm, wc_hbm, out_ref,
    own, stage, kv, bias, q_ref, qe, feat, wo, wc, acc, top, mixed, nrm, halo,
    load_sem, z_send, z_recv, send_sem, near_recv, sib_recv, halo_send, halo_recv,
):
    blk = lax.axis_index("blk")
    tile = lax.axis_index("tile")
    x = blk // 2
    y = lax.rem(blk, 2) * 2 + lax.rem(tile // 2, 2)
    z = tile // 4
    core = lax.rem(tile, 2)
    sib = device(x, y, z, 1 - core)
    me = blk * 32 + tile
    nxt = lax.rem(me + 1, 256)
    prv = lax.rem(me + 255, 256)
    nxt_id = (nxt // 32, lax.rem(nxt, 32))
    prv_id = (prv // 32, lax.rem(prv, 32))
    side = 1 - 2 * core

    loads = [
        pltpu.make_async_copy(k_hbm, own.at[0], load_sem.at[0]),
        pltpu.make_async_copy(v_hbm, own.at[1], load_sem.at[1]),
        pltpu.make_async_copy(q_hbm, q_ref, load_sem.at[2]),
        pltpu.make_async_copy(feat_hbm, feat, load_sem.at[3]),
        pltpu.make_async_copy(wo_hbm, wo, load_sem.at[4]),
        pltpu.make_async_copy(wc_hbm, wc, load_sem.at[5]),
    ]
    loads[0].start()
    loads[1].start()

    barrier = pltpu.get_barrier_semaphore()

    def greet(dev):
        pl.semaphore_signal(barrier, inc=1, device_id=dev, device_id_type=MESH)

    greet(sib)
    for dz in range(1, NZ):
        for c in range(2):
            greet(device(x, y, ring(z + dz, NZ), c))
    for d in (1, 3):
        greet(device(ring(x + d, NX), y, z, core))
        greet(device(x, ring(y + d, NY), z, core))
    greet(nxt_id)
    greet(prv_id)
    for load in loads[2:]:
        load.start()
    loads[0].wait()
    loads[1].wait()
    pl.semaphore_wait(barrier, 21)

    def z_copy(dz, c):
        return pltpu.make_async_remote_copy(
            src_ref=own.at[c],
            dst_ref=stage.at[z, core],
            send_sem=z_send.at[dz, c],
            recv_sem=z_recv.at[z, core],
            device_id=device(x, y, ring(z + dz, NZ), c),
            device_id_type=MESH,
        )

    for dz in (4, 3, 5, 2, 6, 1, 7):
        for c in range(2):
            z_copy(dz, c).start()
    sib_copy = pltpu.make_async_remote_copy(
        src_ref=own.at[1 - core],
        dst_ref=stage.at[z, core],
        send_sem=z_send.at[0, 0],
        recv_sem=z_recv.at[z, core],
        device_id=sib,
        device_id_type=MESH,
    )
    sib_copy.start()
    stage[z, core] = own[core]

    loads[2].wait()
    lane = lax.broadcasted_iota(jnp.int32, (ROWS, 128), 1)
    row = lax.broadcasted_iota(jnp.int32, (ROWS, 128), 0)
    onehot = jnp.where(lane == row // LON, 1.0, 0.0).astype(BF16)
    for p in range(PAIRS):
        part = q_ref[:, p * 128 : (p + 1) * 128].astype(F32) * 0.125
        qe[p, :ROWS, :128] = jnp.where(lane < 64, part, 0.0).astype(BF16)
        qe[p, ROWS:, :128] = jnp.where(lane >= 64, part, 0.0).astype(BF16)
        qe[p, :ROWS, 128:] = onehot
        qe[p, ROWS:, 128:] = onehot

    key = lax.broadcasted_iota(jnp.int32, (128, 128), 0)
    col = lax.broadcasted_iota(jnp.int32, (128, 128), 1)
    low = key < 64

    def mask_block(i, carry):
        kx, ky = i // NY, lax.rem(i, NY)
        b0 = kx * 4 + (ky // 2) * 2
        b1 = b0 + 1
        place = ((key >> 4) & 3) * 32 + (key & 15) + lax.rem(ky, 2) * 16
        limit = jnp.where(low, valid_ref[b0], valid_ref[b1])
        first = jnp.where(low, mask_ref[0, b0], mask_ref[0, b1])
        second = jnp.where(low, mask_ref[1, b0], mask_ref[1, b1])
        wanted = jnp.where(col == 0, first, second)
        live = jnp.where(place < limit, wanted, 0)
        live = jnp.where(col < 2, live, 1)
        bias[kx, ky] = jnp.where(live > 0, 0.0, NEG).astype(BF16)
        return carry

    lax.fori_loop(0, NX * NY, mask_block, 0)

    for dz in range(NZ):
        for c in range(2):
            src_z = ring(z + dz, NZ)

            def arrival(cc):
                return pltpu.make_async_remote_copy(
                    src_ref=own.at[0],
                    dst_ref=stage.at[src_z, cc],
                    send_sem=z_send.at[0, 1],
                    recv_sem=z_recv.at[src_z, cc],
                    device_id=sib,
                    device_id_type=MESH,
                )

            if dz == 0:
                if c == 0:
                    arrival(1 - core).wait_recv()
            else:
                arrival(c).wait_recv()
    block = stage[...].astype(F32).reshape(128, D).astype(BF16)

    uv = ((x, y), (y, x))
    for half in range(2):
        u, v = uv[half]
        kv[core, half, u, v] = block[:, half * 256 : (half + 1) * 256]

    def dev_of(half, u, v, c):
        return device(u, v, z, c) if half == 0 else device(v, u, z, c)

    slots = {}

    def copy_block(half, bu, bv, name, target, recv):
        slot = slots.setdefault((half, name), len(slots))
        return pltpu.make_async_remote_copy(
            src_ref=kv.at[core, half, bu, bv],
            dst_ref=kv.at[core, half, bu, bv],
            send_sem=send_sem.at[slot],
            recv_sem=recv.at[half, bu, bv],
            device_id=target,
            device_id_type=MESH,
        )

    sent = []

    def send(half, bu, bv, name, target, recv=None):
        copy = copy_block(half, bu, bv, name, target, near_recv if recv is None else recv)
        copy.start()
        sent.append(copy)

    def wait_near(half, bu, bv):
        pltpu.make_async_remote_copy(
            src_ref=kv.at[core, half, bu, bv],
            dst_ref=kv.at[core, half, bu, bv],
            send_sem=send_sem.at[0],
            recv_sem=near_recv.at[half, bu, bv],
            device_id=sib,
            device_id_type=MESH,
        ).wait_recv()

    def wait_sib(half, bu, bv):
        pltpu.make_async_remote_copy(
            src_ref=kv.at[1 - core, half, bu, bv],
            dst_ref=kv.at[1 - core, half, bu, bv],
            send_sem=send_sem.at[0],
            recv_sem=sib_recv.at[half, bu, bv],
            device_id=sib,
            device_id_type=MESH,
        ).wait_recv()

    def spread(half, bv, tag):
        u, v = uv[half]
        for d in (1, 3):
            send(half, u, bv, ("u", tag, d), dev_of(half, ring(u + d, 4), v, core))
        send(half, u, bv, ("sib", tag), sib, sib_recv)

    for half in range(2):
        u, v = uv[half]
        for d in (1, 3):
            send(half, u, v, ("v", d), dev_of(half, u, ring(v + d, 4), core))
    for half in range(2):
        spread(half, uv[half][1], 0)
    for half in range(2):
        u, v = uv[half]
        back = ring(v - side, 4)
        wait_near(half, u, back)
        send(half, u, back, ("v", "relay"), dev_of(half, u, ring(v + side, 4), core))
        spread(half, back, 1)
    for half in range(2):
        u, v = uv[half]
        ahead = ring(v + side, 4)
        wait_near(half, u, ahead)
        spread(half, ahead, 2)
    for half in range(2):
        u, v = uv[half]
        far = ring(v + 2, 4)
        wait_near(half, u, far)
        spread(half, far, 3)

    ones = jnp.ones((512, 128), BF16)

    def attend(half, bu, first):
        def one_pair(p, carry):
            pair = half * 2 + p
            cols = pl.ds(pl.multiple_of(p * 128, 128), 128)
            keys = kv[0, half, bu, :, :, cols].reshape(512, 128)
            values = kv[1, half, bu, :, :, cols].reshape(512, 128)
            if half == 0:
                shut = bias[bu].reshape(512, 128)
            else:
                shut = bias[:, bu].reshape(512, 128)
            scores = lax.dot_general(
                qe[pair],
                jnp.concatenate([keys, shut], axis=1),
                (((1,), (1,)), ((), ())),
                preferred_element_type=F32,
            )
            peak = jnp.max(scores, axis=1, keepdims=True)
            if first:
                new_top = jnp.broadcast_to(peak, (512, 128))
            else:
                old_top = top[pair]
                new_top = jnp.maximum(old_top, peak)
            weights = jnp.exp(scores - jnp.concatenate([new_top] * 4, axis=1)).astype(BF16)
            part = jnp.dot(
                weights, jnp.concatenate([values, ones], axis=1), preferred_element_type=F32
            )
            if first:
                acc[pair] = part
            else:
                factor = jnp.exp(old_top - new_top)
                acc[pair] = acc[pair] * jnp.concatenate([factor] * 2, axis=1) + part
            top[pair] = new_top
            return carry

        lax.fori_loop(0, 2, one_pair, 0)

    order = [lambda w: w, lambda w: ring(w - side, 4), lambda w: ring(w + side, 4), lambda w: ring(w + 2, 4)]
    vorder = order

    for half in range(2):
        u, v = uv[half]
        for f in vorder:
            wait_sib(half, u, f(v))
        attend(half, u, True)

    for half in range(2):
        u, v = uv[half]
        bu = order[1](u)
        for i, f in enumerate(vorder):
            wait_near(half, bu, f(v))
            send(half, bu, f(v), ("relay", i), dev_of(half, ring(u + side, 4), v, core))
            send(half, bu, f(v), ("sib1", i), sib, sib_recv)
    for half in range(2):
        u, v = uv[half]
        bu = order[2](u)
        for i, f in enumerate(vorder):
            wait_near(half, bu, f(v))
            send(half, bu, f(v), ("sib2", i), sib, sib_recv)
    for step in (1, 2):
        for half in range(2):
            u, v = uv[half]
            bu = order[step](u)
            for f in vorder:
                wait_sib(half, bu, f(v))
            attend(half, bu, False)
    for half in range(2):
        u, v = uv[half]
        bu = order[3](u)
        for i, f in enumerate(vorder):
            wait_near(half, bu, f(v))
            send(half, bu, f(v), ("sib3", i), sib, sib_recv)
    for half in range(2):
        u, v = uv[half]
        bu = order[3](u)
        for f in vorder:
            wait_sib(half, bu, f(v))
        attend(half, bu, False)

    for pair in range(PAIRS):
        even = acc[pair, :ROWS, :128] / acc[pair, :ROWS, 128:]
        odd = acc[pair, ROWS:, :128] / acc[pair, ROWS:, 128:]
        mixed[:, pair * 128 : (pair + 1) * 128] = jnp.where(lane < 64, even, odd).astype(BF16)

    loads[3].wait()
    loads[4].wait()
    projected = jnp.dot(mixed[...], wo[...], preferred_element_type=F32)
    hidden = (feat[...].astype(F32) + projected).astype(BF16)
    wide = hidden.astype(F32)
    feat[...] = hidden
    normed = (wide * lax.rsqrt(jnp.mean(wide * wide, axis=-1, keepdims=True) + 1e-06)).astype(BF16)
    nrm[...] = normed.reshape(2, LON, D)

    up = pltpu.make_async_remote_copy(
        src_ref=nrm.at[0], dst_ref=halo.at[1], send_sem=halo_send.at[0],
        recv_sem=halo_recv.at[1], device_id=prv_id, device_id_type=MESH,
    )
    down = pltpu.make_async_remote_copy(
        src_ref=nrm.at[1], dst_ref=halo.at[0], send_sem=halo_send.at[1],
        recv_sem=halo_recv.at[0], device_id=nxt_id, device_id_type=MESH,
    )
    up.start()
    down.start()

    def neighbours(field):
        wide_field = field.astype(F32)
        left = pltpu.roll(wide_field, 1, 0).astype(BF16)
        right = pltpu.roll(wide_field, LON - 1, 0).astype(BF16)
        return jnp.concatenate([left, field, right], axis=1)

    loads[5].wait()
    both = jnp.concatenate([neighbours(nrm[0]), neighbours(nrm[1])], axis=1)
    top_row = jnp.dot(both, wc[1:3].reshape(6 * D, D), preferred_element_type=F32)
    low_row = jnp.dot(both, wc[0:2].reshape(6 * D, D), preferred_element_type=F32)

    down.wait_recv()
    above = jnp.where(me > 0, halo[0].astype(F32), 0.0).astype(BF16)
    top_row = top_row + jnp.dot(
        neighbours(above), wc[0].reshape(3 * D, D), preferred_element_type=F32
    )
    out_ref[:LON] = (feat[:LON].astype(F32) + top_row).astype(BF16)
    up.wait_recv()
    below = jnp.where(me < 255, halo[1].astype(F32), 0.0).astype(BF16)
    low_row = low_row + jnp.dot(
        neighbours(below), wc[2].reshape(3 * D, D), preferred_element_type=F32
    )
    out_ref[LON:] = (feat[LON:].astype(F32) + low_row).astype(BF16)

    for dz in range(1, NZ):
        for c in range(2):
            z_copy(dz, c).wait_send()
    sib_copy.wait_send()
    for copy in sent:
        copy.wait_send()
    up.wait_send()
    down.wait_send()


def on_device(grid_feat, queries, obs_keys, obs_values, block_mask, obs_valid, out_weight, conv_weight):
    hbm = pl.BlockSpec(memory_space=pl.ANY)
    smem = pl.BlockSpec(memory_space=pltpu.SMEM)
    return pl.pallas_call(
        kernel,
        out_shape=jax.ShapeDtypeStruct((ROWS, D), BF16),
        in_specs=[smem, smem] + [hbm] * 6,
        out_specs=pl.BlockSpec(memory_space=pltpu.VMEM),
        scratch_shapes=[
            pltpu.VMEM((2, 8, D), BF16),
            pltpu.VMEM((NZ, 2, 8, D), BF16),
            pltpu.VMEM((2, 2, 4, 4, 128, 256), BF16),
            pltpu.VMEM((NX, NY, 128, 128), BF16),
            pltpu.VMEM((ROWS, D), BF16),
            pltpu.VMEM((PAIRS, 512, 256), BF16),
            pltpu.VMEM((ROWS, D), BF16),
            pltpu.VMEM((D, D), BF16),
            pltpu.VMEM((3, 3, D, D), BF16),
            pltpu.VMEM((PAIRS, 512, 256), F32),
            pltpu.VMEM((PAIRS, 512, 128), F32),
            pltpu.VMEM((ROWS, D), BF16),
            pltpu.VMEM((2, LON, D), BF16),
            pltpu.VMEM((2, LON, D), BF16),
            pltpu.SemaphoreType.DMA((6,)),
            pltpu.SemaphoreType.DMA((NZ, 2)),
            pltpu.SemaphoreType.DMA((NZ, 2)),
            pltpu.SemaphoreType.DMA((64,)),
            pltpu.SemaphoreType.DMA((2, 4, 4)),
            pltpu.SemaphoreType.DMA((2, 4, 4)),
            pltpu.SemaphoreType.DMA((2,)),
            pltpu.SemaphoreType.DMA((2,)),
        ],
        compiler_params=pltpu.CompilerParams(
            collective_id=0, has_side_effects=True, vmem_limit_bytes=48 * 1024 * 1024
        ),
    )(block_mask, obs_valid, grid_feat, queries, obs_keys, obs_values, out_weight, conv_weight)


def solution(mesh):
    rows = P(("blk", "tile"), None)
    return jax.shard_map(
        on_device,
        mesh=mesh,
        in_specs=(rows, rows, rows, rows, rows, P(), P(), P()),
        out_specs=rows,
        check_vma=False,
    )
```

```python
import jax
import jax.numpy as jnp
from jax import lax
from jax.experimental import pallas as pl
from jax.experimental.pallas import tpu as pltpu
from jax.sharding import PartitionSpec as P

MESH = pl.DeviceIdType.MESH
NX, NY, NZ = 4, 4, 8
LON = 128
D = 512
ROWS = 256
PAIRS = 4
NEG = -1e30
F32 = jnp.float32
BF16 = jnp.bfloat16


def ring(i, n):
    return lax.rem(i + n, n)


def device(x, y, z, core):
    return (x * 2 + y // 2, z * 4 + lax.rem(y, 2) * 2 + core)


def kernel(
    mask_hbm, valid_hbm, feat_hbm, q_hbm, k_hbm, v_hbm, wo_hbm, wc_hbm, out_ref,
    mask_ref, valid_ref, own, stage, kv, bias, q_ref, qe, feat, wo, wc, acc, top, mixed, nrm, halo,
    load_sem, z_send, z_recv, send_sem, near_recv, sib_recv, halo_send, halo_recv,
):
    blk = lax.axis_index("blk")
    tile = lax.axis_index("tile")
    x = blk // 2
    y = lax.rem(blk, 2) * 2 + lax.rem(tile // 2, 2)
    z = tile // 4
    core = lax.rem(tile, 2)
    sib = device(x, y, z, 1 - core)
    me = blk * 32 + tile
    nxt = lax.rem(me + 1, 256)
    prv = lax.rem(me + 255, 256)
    nxt_id = (nxt // 32, lax.rem(nxt, 32))
    prv_id = (prv // 32, lax.rem(prv, 32))
    side = 1 - 2 * core

    loads = [
        pltpu.make_async_copy(k_hbm, own.at[0], load_sem.at[0]),
        pltpu.make_async_copy(v_hbm, own.at[1], load_sem.at[1]),
        pltpu.make_async_copy(q_hbm, q_ref, load_sem.at[2]),
        pltpu.make_async_copy(feat_hbm, feat, load_sem.at[3]),
        pltpu.make_async_copy(wo_hbm, wo, load_sem.at[4]),
        pltpu.make_async_copy(wc_hbm, wc, load_sem.at[5]),
        pltpu.make_async_copy(mask_hbm, mask_ref, load_sem.at[6]),
        pltpu.make_async_copy(valid_hbm, valid_ref, load_sem.at[7]),
    ]
    loads[0].start()
    loads[1].start()

    barrier = pltpu.get_barrier_semaphore()

    def greet(dev):
        pl.semaphore_signal(barrier, inc=1, device_id=dev, device_id_type=MESH)

    greet(sib)
    for dz in range(1, NZ):
        for c in range(2):
            greet(device(x, y, ring(z + dz, NZ), c))
    for d in (1, 3):
        greet(device(ring(x + d, NX), y, z, core))
        greet(device(x, ring(y + d, NY), z, core))
    greet(nxt_id)
    greet(prv_id)
    for load in loads[2:]:
        load.start()
    loads[0].wait()
    loads[1].wait()
    pl.semaphore_wait(barrier, 21)

    def z_copy(dz, c):
        return pltpu.make_async_remote_copy(
            src_ref=own.at[c],
            dst_ref=stage.at[z, core],
            send_sem=z_send.at[dz, c],
            recv_sem=z_recv.at[z, core],
            device_id=device(x, y, ring(z + dz, NZ), c),
            device_id_type=MESH,
        )

    for dz in (4, 3, 5, 2, 6, 1, 7):
        for c in range(2):
            z_copy(dz, c).start()
    sib_copy = pltpu.make_async_remote_copy(
        src_ref=own.at[1 - core],
        dst_ref=stage.at[z, core],
        send_sem=z_send.at[0, 0],
        recv_sem=z_recv.at[z, core],
        device_id=sib,
        device_id_type=MESH,
    )
    sib_copy.start()
    stage[z, core] = own[core]

    loads[2].wait()
    lane = lax.broadcasted_iota(jnp.int32, (ROWS, 128), 1)
    row = lax.broadcasted_iota(jnp.int32, (ROWS, 128), 0)
    onehot = jnp.where(lane == row // LON, 1.0, 0.0).astype(BF16)
    for p in range(PAIRS):
        part = q_ref[:, p * 128 : (p + 1) * 128].astype(F32) * 0.125
        qe[p, :ROWS, :128] = jnp.where(lane < 64, part, 0.0).astype(BF16)
        qe[p, ROWS:, :128] = jnp.where(lane >= 64, part, 0.0).astype(BF16)
        qe[p, :ROWS, 128:] = onehot
        qe[p, ROWS:, 128:] = onehot

    key = lax.broadcasted_iota(jnp.int32, (128, 128), 0)
    col = lax.broadcasted_iota(jnp.int32, (128, 128), 1)
    low = key < 64

    loads[6].wait()
    loads[7].wait()

    def mask_block(i, carry):
        kx, ky = i // NY, lax.rem(i, NY)
        b0 = kx * 4 + (ky // 2) * 2
        b1 = b0 + 1
        place = ((key >> 4) & 3) * 32 + (key & 15) + lax.rem(ky, 2) * 16
        limit = jnp.where(low, valid_ref[b0], valid_ref[b1])
        first = jnp.where(low, mask_ref[0, b0], mask_ref[0, b1])
        second = jnp.where(low, mask_ref[1, b0], mask_ref[1, b1])
        wanted = jnp.where(col == 0, first, second)
        live = jnp.where(place < limit, wanted, 0)
        live = jnp.where(col < 2, live, 1)
        bias[kx, ky] = jnp.where(live > 0, 0.0, NEG).astype(BF16)
        return carry

    lax.fori_loop(0, NX * NY, mask_block, 0)

    for dz in range(NZ):
        for c in range(2):
            src_z = ring(z + dz, NZ)

            def arrival(cc):
                return pltpu.make_async_remote_copy(
                    src_ref=own.at[0],
                    dst_ref=stage.at[src_z, cc],
                    send_sem=z_send.at[0, 1],
                    recv_sem=z_recv.at[src_z, cc],
                    device_id=sib,
                    device_id_type=MESH,
                )

            if dz == 0:
                if c == 0:
                    arrival(1 - core).wait_recv()
            else:
                arrival(c).wait_recv()
    block = stage[...].astype(F32).reshape(128, D).astype(BF16)

    uv = ((x, y), (y, x))
    for half in range(2):
        u, v = uv[half]
        kv[core, half, u, v] = block[:, half * 256 : (half + 1) * 256]

    def dev_of(half, u, v, c):
        return device(u, v, z, c) if half == 0 else device(v, u, z, c)

    slots = {}

    def copy_block(half, bu, bv, name, target, recv):
        slot = slots.setdefault((half, name), len(slots))
        return pltpu.make_async_remote_copy(
            src_ref=kv.at[core, half, bu, bv],
            dst_ref=kv.at[core, half, bu, bv],
            send_sem=send_sem.at[slot],
            recv_sem=recv.at[half, bu, bv],
            device_id=target,
            device_id_type=MESH,
        )

    sent = []

    def send(half, bu, bv, name, target, recv=None):
        copy = copy_block(half, bu, bv, name, target, near_recv if recv is None else recv)
        copy.start()
        sent.append(copy)

    def wait_near(half, bu, bv):
        pltpu.make_async_remote_copy(
            src_ref=kv.at[core, half, bu, bv],
            dst_ref=kv.at[core, half, bu, bv],
            send_sem=send_sem.at[0],
            recv_sem=near_recv.at[half, bu, bv],
            device_id=sib,
            device_id_type=MESH,
        ).wait_recv()

    def wait_sib(half, bu, bv):
        pltpu.make_async_remote_copy(
            src_ref=kv.at[1 - core, half, bu, bv],
            dst_ref=kv.at[1 - core, half, bu, bv],
            send_sem=send_sem.at[0],
            recv_sem=sib_recv.at[half, bu, bv],
            device_id=sib,
            device_id_type=MESH,
        ).wait_recv()

    def spread(half, bv, tag):
        u, v = uv[half]
        for d in (1, 3):
            send(half, u, bv, ("u", tag, d), dev_of(half, ring(u + d, 4), v, core))
        send(half, u, bv, ("sib", tag), sib, sib_recv)

    for half in range(2):
        u, v = uv[half]
        for d in (1, 3):
            send(half, u, v, ("v", d), dev_of(half, u, ring(v + d, 4), core))
    for half in range(2):
        spread(half, uv[half][1], 0)
    for half in range(2):
        u, v = uv[half]
        back = ring(v - side, 4)
        wait_near(half, u, back)
        send(half, u, back, ("v", "relay"), dev_of(half, u, ring(v + side, 4), core))
        spread(half, back, 1)
    for half in range(2):
        u, v = uv[half]
        ahead = ring(v + side, 4)
        wait_near(half, u, ahead)
        spread(half, ahead, 2)
    for half in range(2):
        u, v = uv[half]
        far = ring(v + 2, 4)
        wait_near(half, u, far)
        spread(half, far, 3)

    ones = jnp.ones((512, 128), BF16)

    def attend(half, bu, first):
        def one_pair(p, carry):
            pair = half * 2 + p
            cols = pl.ds(pl.multiple_of(p * 128, 128), 128)
            keys = kv[0, half, bu, :, :, cols].reshape(512, 128)
            values = kv[1, half, bu, :, :, cols].reshape(512, 128)
            if half == 0:
                shut = bias[bu].reshape(512, 128)
            else:
                shut = bias[:, bu].reshape(512, 128)
            scores = lax.dot_general(
                qe[pair],
                jnp.concatenate([keys, shut], axis=1),
                (((1,), (1,)), ((), ())),
                preferred_element_type=F32,
            )
            peak = jnp.max(scores, axis=1, keepdims=True)
            if first:
                new_top = jnp.broadcast_to(peak, (512, 128))
            else:
                old_top = top[pair]
                new_top = jnp.maximum(old_top, peak)
            weights = jnp.exp(scores - jnp.concatenate([new_top] * 4, axis=1)).astype(BF16)
            part = jnp.dot(
                weights, jnp.concatenate([values, ones], axis=1), preferred_element_type=F32
            )
            if first:
                acc[pair] = part
            else:
                factor = jnp.exp(old_top - new_top)
                acc[pair] = acc[pair] * jnp.concatenate([factor] * 2, axis=1) + part
            top[pair] = new_top
            return carry

        lax.fori_loop(0, 2, one_pair, 0)

    order = [lambda w: w, lambda w: ring(w - side, 4), lambda w: ring(w + side, 4), lambda w: ring(w + 2, 4)]
    vorder = order

    for half in range(2):
        u, v = uv[half]
        for f in vorder:
            wait_sib(half, u, f(v))
        attend(half, u, True)

    for half in range(2):
        u, v = uv[half]
        bu = order[1](u)
        for i, f in enumerate(vorder):
            wait_near(half, bu, f(v))
            send(half, bu, f(v), ("relay", i), dev_of(half, ring(u + side, 4), v, core))
            send(half, bu, f(v), ("sib1", i), sib, sib_recv)
    for half in range(2):
        u, v = uv[half]
        bu = order[2](u)
        for i, f in enumerate(vorder):
            wait_near(half, bu, f(v))
            send(half, bu, f(v), ("sib2", i), sib, sib_recv)
    for step in (1, 2):
        for half in range(2):
            u, v = uv[half]
            bu = order[step](u)
            for f in vorder:
                wait_sib(half, bu, f(v))
            attend(half, bu, False)
    for half in range(2):
        u, v = uv[half]
        bu = order[3](u)
        for i, f in enumerate(vorder):
            wait_near(half, bu, f(v))
            send(half, bu, f(v), ("sib3", i), sib, sib_recv)
    for half in range(2):
        u, v = uv[half]
        bu = order[3](u)
        for f in vorder:
            wait_sib(half, bu, f(v))
        attend(half, bu, False)

    for pair in range(PAIRS):
        even = acc[pair, :ROWS, :128] / acc[pair, :ROWS, 128:]
        odd = acc[pair, ROWS:, :128] / acc[pair, ROWS:, 128:]
        mixed[:, pair * 128 : (pair + 1) * 128] = jnp.where(lane < 64, even, odd).astype(BF16)

    loads[3].wait()
    loads[4].wait()
    projected = jnp.dot(mixed[...], wo[...], preferred_element_type=F32)
    hidden = (feat[...].astype(F32) + projected).astype(BF16)
    wide = hidden.astype(F32)
    feat[...] = hidden
    normed = (wide * lax.rsqrt(jnp.mean(wide * wide, axis=-1, keepdims=True) + 1e-06)).astype(BF16)
    nrm[...] = normed.reshape(2, LON, D)

    up = pltpu.make_async_remote_copy(
        src_ref=nrm.at[0], dst_ref=halo.at[1], send_sem=halo_send.at[0],
        recv_sem=halo_recv.at[1], device_id=prv_id, device_id_type=MESH,
    )
    down = pltpu.make_async_remote_copy(
        src_ref=nrm.at[1], dst_ref=halo.at[0], send_sem=halo_send.at[1],
        recv_sem=halo_recv.at[0], device_id=nxt_id, device_id_type=MESH,
    )
    up.start()
    down.start()

    def neighbours(field):
        wide_field = field.astype(F32)
        left = pltpu.roll(wide_field, 1, 0).astype(BF16)
        right = pltpu.roll(wide_field, LON - 1, 0).astype(BF16)
        return jnp.concatenate([left, field, right], axis=1)

    loads[5].wait()
    both = jnp.concatenate([neighbours(nrm[0]), neighbours(nrm[1])], axis=1)
    top_row = jnp.dot(both, wc[1:3].reshape(6 * D, D), preferred_element_type=F32)
    low_row = jnp.dot(both, wc[0:2].reshape(6 * D, D), preferred_element_type=F32)

    down.wait_recv()
    above = jnp.where(me > 0, halo[0].astype(F32), 0.0).astype(BF16)
    top_row = top_row + jnp.dot(
        neighbours(above), wc[0].reshape(3 * D, D), preferred_element_type=F32
    )
    out_ref[:LON] = (feat[:LON].astype(F32) + top_row).astype(BF16)
    up.wait_recv()
    below = jnp.where(me < 255, halo[1].astype(F32), 0.0).astype(BF16)
    low_row = low_row + jnp.dot(
        neighbours(below), wc[2].reshape(3 * D, D), preferred_element_type=F32
    )
    out_ref[LON:] = (feat[LON:].astype(F32) + low_row).astype(BF16)

    for dz in range(1, NZ):
        for c in range(2):
            z_copy(dz, c).wait_send()
    sib_copy.wait_send()
    for copy in sent:
        copy.wait_send()
    up.wait_send()
    down.wait_send()


def on_device(grid_feat, queries, obs_keys, obs_values, block_mask, obs_valid, out_weight, conv_weight):
    hbm = pl.BlockSpec(memory_space=pltpu.HBM)
    return pl.pallas_call(
        kernel,
        out_shape=jax.ShapeDtypeStruct((ROWS, D), BF16),
        in_specs=[hbm] * 8,
        out_specs=pl.BlockSpec(memory_space=pltpu.VMEM),
        scratch_shapes=[
            pltpu.SMEM((2, 16), jnp.int32),
            pltpu.SMEM((16,), jnp.int32),
            pltpu.VMEM((2, 8, D), BF16),
            pltpu.VMEM((NZ, 2, 8, D), BF16),
            pltpu.VMEM((2, 2, 4, 4, 128, 256), BF16),
            pltpu.VMEM((NX, NY, 128, 128), BF16),
            pltpu.VMEM((ROWS, D), BF16),
            pltpu.VMEM((PAIRS, 512, 256), BF16),
            pltpu.VMEM((ROWS, D), BF16),
            pltpu.VMEM((D, D), BF16),
            pltpu.VMEM((3, 3, D, D), BF16),
            pltpu.VMEM((PAIRS, 512, 256), F32),
            pltpu.VMEM((PAIRS, 512, 128), F32),
            pltpu.VMEM((ROWS, D), BF16),
            pltpu.VMEM((2, LON, D), BF16),
            pltpu.VMEM((2, LON, D), BF16),
            pltpu.SemaphoreType.DMA((8,)),
            pltpu.SemaphoreType.DMA((NZ, 2)),
            pltpu.SemaphoreType.DMA((NZ, 2)),
            pltpu.SemaphoreType.DMA((64,)),
            pltpu.SemaphoreType.DMA((2, 4, 4)),
            pltpu.SemaphoreType.DMA((2, 4, 4)),
            pltpu.SemaphoreType.DMA((2,)),
            pltpu.SemaphoreType.DMA((2,)),
        ],
        compiler_params=pltpu.CompilerParams(
            collective_id=0, has_side_effects=True, vmem_limit_bytes=58 * 1024 * 1024
        ),
    )(block_mask, obs_valid, grid_feat, queries, obs_keys, obs_values, out_weight, conv_weight)


def solution(mesh):
    rows = P(("blk", "tile"), None)
    return jax.shard_map(
        on_device,
        mesh=mesh,
        in_specs=(rows, rows, rows, rows, rows, P(), P(), P()),
        out_specs=rows,
        check_vma=False,
    )
```

```python
import jax
import jax.numpy as jnp
from jax import lax
from jax.experimental import pallas as pl
from jax.experimental.pallas import tpu as pltpu
from jax.sharding import PartitionSpec as P

MESH = pl.DeviceIdType.MESH
NX, NY, NZ = 4, 4, 8
LON = 128
D = 512
ROWS = 256
PAIRS = 4
NEG = -1e30
F32 = jnp.float32
BF16 = jnp.bfloat16


def ring(i, n):
    return lax.rem(i + n, n)


def device(x, y, z, core):
    return (x * 2 + y // 2, z * 4 + lax.rem(y, 2) * 2 + core)


def kernel(
    mask_hbm, valid_hbm, feat_hbm, q_hbm, k_hbm, v_hbm, wo_hbm, wc_hbm, out_ref,
    mask_ref, valid_ref, own, stage, kv, bias, q_ref, qt, feat, wo, wc, acc, top, mixed, nrm, halo,
    load_sem, z_send, z_recv, send_sem, near_recv, sib_recv, halo_send, halo_recv,
):
    blk = lax.axis_index("blk")
    tile = lax.axis_index("tile")
    x = blk // 2
    y = lax.rem(blk, 2) * 2 + lax.rem(tile // 2, 2)
    z = tile // 4
    core = lax.rem(tile, 2)
    sib = device(x, y, z, 1 - core)
    me = blk * 32 + tile
    nxt = lax.rem(me + 1, 256)
    prv = lax.rem(me + 255, 256)
    nxt_id = (nxt // 32, lax.rem(nxt, 32))
    prv_id = (prv // 32, lax.rem(prv, 32))
    side = 1 - 2 * core

    loads = [
        pltpu.make_async_copy(k_hbm, own.at[0], load_sem.at[0]),
        pltpu.make_async_copy(v_hbm, own.at[1], load_sem.at[1]),
        pltpu.make_async_copy(q_hbm, q_ref, load_sem.at[2]),
        pltpu.make_async_copy(feat_hbm, feat, load_sem.at[3]),
        pltpu.make_async_copy(wo_hbm, wo, load_sem.at[4]),
        pltpu.make_async_copy(wc_hbm, wc, load_sem.at[5]),
        pltpu.make_async_copy(mask_hbm, mask_ref, load_sem.at[6]),
        pltpu.make_async_copy(valid_hbm, valid_ref, load_sem.at[7]),
    ]
    loads[0].start()
    loads[1].start()

    barrier = pltpu.get_barrier_semaphore()

    def greet(dev):
        pl.semaphore_signal(barrier, inc=1, device_id=dev, device_id_type=MESH)

    greet(sib)
    for dz in range(1, NZ):
        for c in range(2):
            greet(device(x, y, ring(z + dz, NZ), c))
    for d in (1, 3):
        greet(device(ring(x + d, NX), y, z, core))
        greet(device(x, ring(y + d, NY), z, core))
    greet(nxt_id)
    greet(prv_id)
    for load in loads[2:]:
        load.start()
    loads[0].wait()
    loads[1].wait()
    pl.semaphore_wait(barrier, 21)

    def z_copy(dz, c):
        return pltpu.make_async_remote_copy(
            src_ref=own.at[c],
            dst_ref=stage.at[z, core],
            send_sem=z_send.at[dz, c],
            recv_sem=z_recv.at[z, core],
            device_id=device(x, y, ring(z + dz, NZ), c),
            device_id_type=MESH,
        )

    for dz in (4, 3, 5, 2, 6, 1, 7):
        for c in range(2):
            z_copy(dz, c).start()
    sib_copy = pltpu.make_async_remote_copy(
        src_ref=own.at[1 - core],
        dst_ref=stage.at[z, core],
        send_sem=z_send.at[0, 0],
        recv_sem=z_recv.at[z, core],
        device_id=sib,
        device_id_type=MESH,
    )
    sib_copy.start()
    stage[z, core] = own[core]

    loads[2].wait()
    feat_row = lax.broadcasted_iota(jnp.int32, (128, ROWS), 0)
    query_col = lax.broadcasted_iota(jnp.int32, (128, ROWS), 1)
    onehot = jnp.where(feat_row == query_col // LON, 1.0, 0.0).astype(BF16)
    for p in range(PAIRS):
        part = (q_ref[:, p * 128 : (p + 1) * 128].astype(F32) * 0.125).T
        qt[p, :128, :ROWS] = jnp.where(feat_row < 64, part, 0.0).astype(BF16)
        qt[p, :128, ROWS:] = jnp.where(feat_row >= 64, part, 0.0).astype(BF16)
        qt[p, 128:, :ROWS] = onehot
        qt[p, 128:, ROWS:] = onehot

    key = lax.broadcasted_iota(jnp.int32, (128, 128), 0)
    col = lax.broadcasted_iota(jnp.int32, (128, 128), 1)
    low = key < 64

    loads[6].wait()
    loads[7].wait()

    def mask_block(i, carry):
        kx, ky = i // NY, lax.rem(i, NY)
        b0 = kx * 4 + (ky // 2) * 2
        b1 = b0 + 1
        place = ((key >> 4) & 3) * 32 + (key & 15) + lax.rem(ky, 2) * 16
        limit = jnp.where(low, valid_ref[b0], valid_ref[b1])
        first = jnp.where(low, mask_ref[0, b0], mask_ref[0, b1])
        second = jnp.where(low, mask_ref[1, b0], mask_ref[1, b1])
        wanted = jnp.where(col == 0, first, second)
        live = jnp.where(place < limit, wanted, 0)
        live = jnp.where(col < 2, live, 1)
        bias[kx, ky] = jnp.where(live > 0, 0.0, NEG).astype(BF16)
        return carry

    lax.fori_loop(0, NX * NY, mask_block, 0)

    for dz in range(NZ):
        for c in range(2):
            src_z = ring(z + dz, NZ)

            def arrival(cc):
                return pltpu.make_async_remote_copy(
                    src_ref=own.at[0],
                    dst_ref=stage.at[src_z, cc],
                    send_sem=z_send.at[0, 1],
                    recv_sem=z_recv.at[src_z, cc],
                    device_id=sib,
                    device_id_type=MESH,
                )

            if dz == 0:
                if c == 0:
                    arrival(1 - core).wait_recv()
            else:
                arrival(c).wait_recv()
    plain = stage[...].astype(F32).reshape(128, D)
    turned = jnp.concatenate([plain[:, p * 128 : (p + 1) * 128].T for p in range(PAIRS)], axis=1)
    block = jnp.where(core == 0, plain, turned).astype(BF16)

    uv = ((x, y), (y, x))
    for half in range(2):
        u, v = uv[half]
        kv[core, half, u, v] = block[:, half * 256 : (half + 1) * 256]

    def dev_of(half, u, v, c):
        return device(u, v, z, c) if half == 0 else device(v, u, z, c)

    slots = {}

    def copy_block(half, bu, bv, name, target, recv):
        slot = slots.setdefault((half, name), len(slots))
        return pltpu.make_async_remote_copy(
            src_ref=kv.at[core, half, bu, bv],
            dst_ref=kv.at[core, half, bu, bv],
            send_sem=send_sem.at[slot],
            recv_sem=recv.at[half, bu, bv],
            device_id=target,
            device_id_type=MESH,
        )

    sent = []

    def send(half, bu, bv, name, target, recv=None):
        copy = copy_block(half, bu, bv, name, target, near_recv if recv is None else recv)
        copy.start()
        sent.append(copy)

    def wait_near(half, bu, bv):
        pltpu.make_async_remote_copy(
            src_ref=kv.at[core, half, bu, bv],
            dst_ref=kv.at[core, half, bu, bv],
            send_sem=send_sem.at[0],
            recv_sem=near_recv.at[half, bu, bv],
            device_id=sib,
            device_id_type=MESH,
        ).wait_recv()

    def wait_sib(half, bu, bv):
        pltpu.make_async_remote_copy(
            src_ref=kv.at[1 - core, half, bu, bv],
            dst_ref=kv.at[1 - core, half, bu, bv],
            send_sem=send_sem.at[0],
            recv_sem=sib_recv.at[half, bu, bv],
            device_id=sib,
            device_id_type=MESH,
        ).wait_recv()

    def spread(half, bv, tag):
        u, v = uv[half]
        for d in (1, 3):
            send(half, u, bv, ("u", tag, d), dev_of(half, ring(u + d, 4), v, core))
        send(half, u, bv, ("sib", tag), sib, sib_recv)

    ones = jnp.ones((16, 512), BF16)

    def attend(half, blocks, first):
        for p in range(2):
            pair = half * 2 + p
            cols = slice(p * 128, (p + 1) * 128)
            keys = [kv[0, half, bu, bv, :, cols] for bu, bv in blocks]
            values = [kv[1, half, bu, bv, :, cols] for bu, bv in blocks]
            shut = [bias[bu, bv] if half == 0 else bias[bv, bu] for bu, bv in blocks]
            scores = jnp.dot(
                jnp.concatenate(
                    [jnp.concatenate(keys, axis=0), jnp.concatenate(shut, axis=0)], axis=1
                ),
                qt[pair],
                preferred_element_type=F32,
            )
            peak = jnp.max(scores, axis=0, keepdims=True)
            if first:
                new_top = jnp.broadcast_to(peak, (8, 512))
            else:
                old_top = top[pair]
                new_top = jnp.maximum(old_top, peak)
            weights = jnp.exp(scores - new_top[:1]).astype(BF16)
            part = jnp.dot(
                jnp.concatenate([jnp.concatenate(values, axis=1), ones], axis=0),
                weights,
                preferred_element_type=F32,
            )
            if first:
                acc[pair] = part
            else:
                factor = jnp.exp(old_top - new_top)
                acc[pair] = acc[pair] * factor[:1] + part
            top[pair] = new_top

    us = []
    vs = []
    for half in range(2):
        u, v = uv[half]
        us.append((u, ring(u - side, 4), ring(u + side, 4), ring(u + 2, 4)))
        vs.append((v, ring(v - side, 4), ring(v + side, 4), ring(v + 2, 4)))
    OWN, BACK, AHEAD, FAR = 0, 1, 2, 3

    def both(step, *args):
        for half in range(2):
            step(half, *args)

    def line_sends(half):
        u, v = uv[half]
        for d in (1, 3):
            send(half, u, v, ("v", d), dev_of(half, u, ring(v + d, 4), core))

    def line_block(half, c):
        u, v = uv[half]
        bv = vs[half][c]
        if c != OWN:
            wait_near(half, u, bv)
        if c == BACK:
            send(half, u, bv, ("v", "relay"), dev_of(half, u, vs[half][AHEAD], core))
        spread(half, bv, c)

    def from_back(half, c):
        bu, bv = us[half][BACK], vs[half][c]
        wait_near(half, bu, bv)
        send(half, bu, bv, ("relay", c), dev_of(half, us[half][AHEAD], uv[half][1], core))
        send(half, bu, bv, ("sib1", c), sib, sib_recv)

    def from_ahead(half, c):
        bu, bv = us[half][AHEAD], vs[half][c]
        wait_near(half, bu, bv)
        send(half, bu, bv, ("sib2", c), sib, sib_recv)

    def from_far(half, c):
        bu, bv = us[half][FAR], vs[half][c]
        wait_near(half, bu, bv)
        send(half, bu, bv, ("sib3", c), sib, sib_recv)

    def chunk(half, places, first=False):
        blocks = [(us[half][a], vs[half][b]) for a, b in places]
        for bu, bv in blocks:
            wait_sib(half, bu, bv)
        attend(half, blocks, first)

    line = [(OWN, c) for c in (OWN, BACK, AHEAD, FAR)]
    close = [(a, c) for a in (BACK, AHEAD) for c in (OWN, BACK)]
    wide_off = [(a, c) for a in (BACK, AHEAD) for c in (AHEAD, FAR)]
    last = [(FAR, c) for c in (OWN, BACK, AHEAD, FAR)]

    both(line_sends)
    both(line_block, OWN)
    both(line_block, BACK)
    both(line_block, AHEAD)
    both(from_back, OWN)
    both(from_ahead, OWN)
    both(line_block, FAR)
    chunk(0, line, True)
    both(from_back, BACK)
    both(from_ahead, BACK)
    chunk(1, line, True)
    both(from_back, AHEAD)
    both(from_ahead, AHEAD)
    both(from_far, OWN)
    both(from_back, FAR)
    both(from_ahead, FAR)
    both(from_far, BACK)
    chunk(0, close)
    chunk(1, close)
    both(from_far, AHEAD)
    chunk(0, wide_off)
    chunk(1, wide_off)
    both(from_far, FAR)
    chunk(0, last)
    chunk(1, last)

    for pair in range(PAIRS):
        share = 1.0 / acc[pair, 128:129, :]
        even = acc[pair, :64, :ROWS] * share[:, :ROWS]
        odd = acc[pair, 64:128, ROWS:] * share[:, ROWS:]
        mixed[:, pair * 128 : (pair + 1) * 128] = jnp.concatenate([even, odd], axis=0).T.astype(BF16)

    loads[3].wait()
    loads[4].wait()
    projected = jnp.dot(mixed[...], wo[...], preferred_element_type=F32)
    hidden = (feat[...].astype(F32) + projected).astype(BF16)
    wide = hidden.astype(F32)
    feat[...] = hidden
    normed = (wide * lax.rsqrt(jnp.mean(wide * wide, axis=-1, keepdims=True) + 1e-06)).astype(BF16)
    nrm[...] = normed.reshape(2, LON, D)

    up = pltpu.make_async_remote_copy(
        src_ref=nrm.at[0], dst_ref=halo.at[1], send_sem=halo_send.at[0],
        recv_sem=halo_recv.at[1], device_id=prv_id, device_id_type=MESH,
    )
    down = pltpu.make_async_remote_copy(
        src_ref=nrm.at[1], dst_ref=halo.at[0], send_sem=halo_send.at[1],
        recv_sem=halo_recv.at[0], device_id=nxt_id, device_id_type=MESH,
    )
    up.start()
    down.start()

    def neighbours(field):
        wide_field = field.astype(F32)
        left = pltpu.roll(wide_field, 1, 0).astype(BF16)
        right = pltpu.roll(wide_field, LON - 1, 0).astype(BF16)
        return jnp.concatenate([left, field, right], axis=1)

    loads[5].wait()
    pair_rows = jnp.concatenate([neighbours(nrm[0]), neighbours(nrm[1])], axis=1)
    top_row = jnp.dot(pair_rows, wc[1:3].reshape(6 * D, D), preferred_element_type=F32)
    low_row = jnp.dot(pair_rows, wc[0:2].reshape(6 * D, D), preferred_element_type=F32)

    down.wait_recv()
    above = jnp.where(me > 0, halo[0].astype(F32), 0.0).astype(BF16)
    top_row = top_row + jnp.dot(
        neighbours(above), wc[0].reshape(3 * D, D), preferred_element_type=F32
    )
    out_ref[:LON] = (feat[:LON].astype(F32) + top_row).astype(BF16)
    up.wait_recv()
    below = jnp.where(me < 255, halo[1].astype(F32), 0.0).astype(BF16)
    low_row = low_row + jnp.dot(
        neighbours(below), wc[2].reshape(3 * D, D), preferred_element_type=F32
    )
    out_ref[LON:] = (feat[LON:].astype(F32) + low_row).astype(BF16)

    for dz in range(1, NZ):
        for c in range(2):
            z_copy(dz, c).wait_send()
    sib_copy.wait_send()
    for copy in sent:
        copy.wait_send()
    up.wait_send()
    down.wait_send()


def on_device(grid_feat, queries, obs_keys, obs_values, block_mask, obs_valid, out_weight, conv_weight):
    hbm = pl.BlockSpec(memory_space=pltpu.HBM)
    return pl.pallas_call(
        kernel,
        out_shape=jax.ShapeDtypeStruct((ROWS, D), BF16),
        in_specs=[hbm] * 8,
        out_specs=pl.BlockSpec(memory_space=pltpu.VMEM),
        scratch_shapes=[
            pltpu.SMEM((2, 16), jnp.int32),
            pltpu.SMEM((16,), jnp.int32),
            pltpu.VMEM((2, 8, D), BF16),
            pltpu.VMEM((NZ, 2, 8, D), BF16),
            pltpu.VMEM((2, 2, 4, 4, 128, 256), BF16),
            pltpu.VMEM((NX, NY, 128, 128), BF16),
            pltpu.VMEM((ROWS, D), BF16),
            pltpu.VMEM((PAIRS, 256, 512), BF16),
            pltpu.VMEM((ROWS, D), BF16),
            pltpu.VMEM((D, D), BF16),
            pltpu.VMEM((3, 3, D, D), BF16),
            pltpu.VMEM((PAIRS, 144, 512), F32),
            pltpu.VMEM((PAIRS, 8, 512), F32),
            pltpu.VMEM((ROWS, D), BF16),
            pltpu.VMEM((2, LON, D), BF16),
            pltpu.VMEM((2, LON, D), BF16),
            pltpu.SemaphoreType.DMA((8,)),
            pltpu.SemaphoreType.DMA((NZ, 2)),
            pltpu.SemaphoreType.DMA((NZ, 2)),
            pltpu.SemaphoreType.DMA((64,)),
            pltpu.SemaphoreType.DMA((2, 4, 4)),
            pltpu.SemaphoreType.DMA((2, 4, 4)),
            pltpu.SemaphoreType.DMA((2,)),
            pltpu.SemaphoreType.DMA((2,)),
        ],
        compiler_params=pltpu.CompilerParams(
            collective_id=0, has_side_effects=True, vmem_limit_bytes=58 * 1024 * 1024
        ),
    )(block_mask, obs_valid, grid_feat, queries, obs_keys, obs_values, out_weight, conv_weight)


def solution(mesh):
    rows = P(("blk", "tile"), None)
    return jax.shard_map(
        on_device,
        mesh=mesh,
        in_specs=(rows, rows, rows, rows, rows, P(), P(), P()),
        out_specs=rows,
        check_vma=False,
    )
```

```python
import jax
import jax.numpy as jnp
from jax import lax
from jax.experimental import pallas as pl
from jax.experimental.pallas import tpu as pltpu
from jax.sharding import PartitionSpec as P

MESH = pl.DeviceIdType.MESH
NX, NY, NZ = 4, 4, 8
LON = 128
D = 512
ROWS = 256
PAIRS = 4
NEG = -1e30
F32 = jnp.float32
BF16 = jnp.bfloat16


def ring(i, n):
    return lax.rem(i + n, n)


def device(x, y, z, core):
    return (x * 2 + y // 2, z * 4 + lax.rem(y, 2) * 2 + core)


def kernel(
    mask_hbm, valid_hbm, feat_hbm, q_hbm, k_hbm, v_hbm, wo_hbm, wc_hbm, out_ref,
    mask_ref, valid_ref, own, stage, kv, bias, q_ref, qt, feat, wo, wc, acc, top, mixed, nrm, halo,
    load_sem, z_send, z_recv, send_sem, near_recv, sib_recv, halo_send, halo_recv,
):
    blk = lax.axis_index("blk")
    tile = lax.axis_index("tile")
    x = blk // 2
    y = lax.rem(blk, 2) * 2 + lax.rem(tile // 2, 2)
    z = tile // 4
    core = lax.rem(tile, 2)
    sib = device(x, y, z, 1 - core)
    me = blk * 32 + tile
    nxt = lax.rem(me + 1, 256)
    prv = lax.rem(me + 255, 256)
    nxt_id = (nxt // 32, lax.rem(nxt, 32))
    prv_id = (prv // 32, lax.rem(prv, 32))
    side = 1 - 2 * core

    loads = [
        pltpu.make_async_copy(k_hbm, own.at[0], load_sem.at[0]),
        pltpu.make_async_copy(v_hbm, own.at[1], load_sem.at[1]),
        pltpu.make_async_copy(q_hbm, q_ref, load_sem.at[2]),
        pltpu.make_async_copy(feat_hbm, feat, load_sem.at[3]),
        pltpu.make_async_copy(wo_hbm, wo, load_sem.at[4]),
        pltpu.make_async_copy(wc_hbm, wc, load_sem.at[5]),
        pltpu.make_async_copy(mask_hbm, mask_ref, load_sem.at[6]),
        pltpu.make_async_copy(valid_hbm, valid_ref, load_sem.at[7]),
    ]
    loads[0].start()
    loads[1].start()

    barrier = pltpu.get_barrier_semaphore()

    def greet(dev):
        pl.semaphore_signal(barrier, inc=1, device_id=dev, device_id_type=MESH)

    greet(sib)
    for dz in range(1, NZ):
        for c in range(2):
            greet(device(x, y, ring(z + dz, NZ), c))
    for d in (1, 2, 3):
        greet(device(ring(x + d, NX), y, z, core))
        greet(device(x, ring(y + d, NY), z, core))
    greet(nxt_id)
    greet(prv_id)
    for load in loads[2:]:
        load.start()
    loads[0].wait()
    loads[1].wait()
    pl.semaphore_wait(barrier, 23)

    def z_copy(dz, c):
        return pltpu.make_async_remote_copy(
            src_ref=own.at[c],
            dst_ref=stage.at[z, core],
            send_sem=z_send.at[dz, c],
            recv_sem=z_recv.at[z, core],
            device_id=device(x, y, ring(z + dz, NZ), c),
            device_id_type=MESH,
        )

    for dz in (4, 3, 5, 2, 6, 1, 7):
        for c in range(2):
            z_copy(dz, c).start()
    sib_copy = pltpu.make_async_remote_copy(
        src_ref=own.at[1 - core],
        dst_ref=stage.at[z, core],
        send_sem=z_send.at[0, 0],
        recv_sem=z_recv.at[z, core],
        device_id=sib,
        device_id_type=MESH,
    )
    sib_copy.start()
    stage[z, core] = own[core]

    loads[2].wait()
    feat_row = lax.broadcasted_iota(jnp.int32, (128, ROWS), 0)
    query_col = lax.broadcasted_iota(jnp.int32, (128, ROWS), 1)
    onehot = jnp.where(feat_row == query_col // LON, 1.0, 0.0).astype(BF16)
    for p in range(PAIRS):
        part = (q_ref[:, p * 128 : (p + 1) * 128].astype(F32) * 0.125).T
        qt[p, :128, :ROWS] = jnp.where(feat_row < 64, part, 0.0).astype(BF16)
        qt[p, :128, ROWS:] = jnp.where(feat_row >= 64, part, 0.0).astype(BF16)
        qt[p, 128:, :ROWS] = onehot
        qt[p, 128:, ROWS:] = onehot

    key = lax.broadcasted_iota(jnp.int32, (128, 128), 0)
    col = lax.broadcasted_iota(jnp.int32, (128, 128), 1)
    low = key < 64

    loads[6].wait()
    loads[7].wait()

    def mask_block(i, carry):
        kx, ky = i // NY, lax.rem(i, NY)
        b0 = kx * 4 + (ky // 2) * 2
        b1 = b0 + 1
        place = ((key >> 4) & 3) * 32 + (key & 15) + lax.rem(ky, 2) * 16
        limit = jnp.where(low, valid_ref[b0], valid_ref[b1])
        first = jnp.where(low, mask_ref[0, b0], mask_ref[0, b1])
        second = jnp.where(low, mask_ref[1, b0], mask_ref[1, b1])
        wanted = jnp.where(col == 0, first, second)
        live = jnp.where(place < limit, wanted, 0)
        live = jnp.where(col < 2, live, 1)
        bias[kx, ky] = jnp.where(live > 0, 0.0, NEG).astype(BF16)
        return carry

    lax.fori_loop(0, NX * NY, mask_block, 0)

    for dz in range(NZ):
        for c in range(2):
            src_z = ring(z + dz, NZ)

            def arrival(cc):
                return pltpu.make_async_remote_copy(
                    src_ref=own.at[0],
                    dst_ref=stage.at[src_z, cc],
                    send_sem=z_send.at[0, 1],
                    recv_sem=z_recv.at[src_z, cc],
                    device_id=sib,
                    device_id_type=MESH,
                )

            if dz == 0:
                if c == 0:
                    arrival(1 - core).wait_recv()
            else:
                arrival(c).wait_recv()
    plain = stage[...].astype(F32).reshape(128, D)
    turned = jnp.concatenate([plain[:, p * 128 : (p + 1) * 128].T for p in range(PAIRS)], axis=1)
    block = jnp.where(core == 0, plain, turned).astype(BF16)

    uv = ((x, y), (y, x))
    for half in range(2):
        u, v = uv[half]
        kv[core, half, u, v] = block[:, half * 256 : (half + 1) * 256]

    def dev_of(half, u, v, c):
        return device(u, v, z, c) if half == 0 else device(v, u, z, c)

    slots = {}

    def copy_block(half, bu, bv, name, target, recv):
        slot = slots.setdefault((half, name), len(slots))
        return pltpu.make_async_remote_copy(
            src_ref=kv.at[core, half, bu, bv],
            dst_ref=kv.at[core, half, bu, bv],
            send_sem=send_sem.at[slot],
            recv_sem=recv.at[half, bu, bv],
            device_id=target,
            device_id_type=MESH,
        )

    sent = []

    def send(half, bu, bv, name, target, recv=None):
        copy = copy_block(half, bu, bv, name, target, near_recv if recv is None else recv)
        copy.start()
        sent.append(copy)

    def wait_near(half, bu, bv):
        pltpu.make_async_remote_copy(
            src_ref=kv.at[core, half, bu, bv],
            dst_ref=kv.at[core, half, bu, bv],
            send_sem=send_sem.at[0],
            recv_sem=near_recv.at[half, bu, bv],
            device_id=sib,
            device_id_type=MESH,
        ).wait_recv()

    def wait_sib(half, bu, bv):
        pltpu.make_async_remote_copy(
            src_ref=kv.at[1 - core, half, bu, bv],
            dst_ref=kv.at[1 - core, half, bu, bv],
            send_sem=send_sem.at[0],
            recv_sem=sib_recv.at[half, bu, bv],
            device_id=sib,
            device_id_type=MESH,
        ).wait_recv()

    def spread(half, bv, tag):
        u, v = uv[half]
        for d in (1, 3):
            send(half, u, bv, ("u", tag, d), dev_of(half, ring(u + d, 4), v, core))
        send(half, u, bv, ("sib", tag), sib, sib_recv)

    ones = jnp.ones((16, 512), BF16)

    def attend(half, blocks, first):
        for p in range(2):
            pair = half * 2 + p
            cols = slice(p * 128, (p + 1) * 128)
            keys = [kv[0, half, bu, bv, :, cols] for bu, bv in blocks]
            values = [kv[1, half, bu, bv, :, cols] for bu, bv in blocks]
            shut = [bias[bu, bv] if half == 0 else bias[bv, bu] for bu, bv in blocks]
            scores = jnp.dot(
                jnp.concatenate(
                    [jnp.concatenate(keys, axis=0), jnp.concatenate(shut, axis=0)], axis=1
                ),
                qt[pair],
                preferred_element_type=F32,
            )
            peak = jnp.max(scores, axis=0, keepdims=True)
            if first:
                new_top = jnp.broadcast_to(peak, (8, 512))
            else:
                old_top = top[pair]
                new_top = jnp.maximum(old_top, peak)
            weights = jnp.exp(scores - new_top[:1]).astype(BF16)
            part = jnp.dot(
                jnp.concatenate([jnp.concatenate(values, axis=1), ones], axis=0),
                weights,
                preferred_element_type=F32,
            )
            if first:
                acc[pair] = part
            else:
                factor = jnp.exp(old_top - new_top)
                acc[pair] = acc[pair] * factor[:1] + part
            top[pair] = new_top

    us = []
    vs = []
    for half in range(2):
        u, v = uv[half]
        us.append((u, ring(u - side, 4), ring(u + side, 4), ring(u + 2, 4)))
        vs.append((v, ring(v + 1, 4), ring(v - 1, 4), ring(v + 2, 4)))
    OWN, NEXT, PREV, FAR = 0, 1, 2, 3
    BACK, AHEAD = 1, 2

    def both(step, *args):
        for half in range(2):
            step(half, *args)

    def line_sends(half):
        u, v = uv[half]
        for d in (1, 3, 2):
            send(half, u, v, ("v", d), dev_of(half, u, ring(v + d, 4), core))

    def line_near(half):
        u, v = uv[half]
        wait_near(half, u, vs[half][NEXT])
        spread(half, vs[half][NEXT], NEXT)
        wait_near(half, u, vs[half][PREV])
        spread(half, vs[half][PREV], PREV)

    def line_far(half):
        wait_near(half, uv[half][0], vs[half][FAR])
        spread(half, vs[half][FAR], FAR)

    def from_back(half, c):
        bu, bv = us[half][BACK], vs[half][c]
        wait_near(half, bu, bv)
        send(half, bu, bv, ("relay", c), dev_of(half, us[half][AHEAD], uv[half][1], core))
        send(half, bu, bv, ("sib1", c), sib, sib_recv)

    def from_ahead(half, c):
        bu, bv = us[half][AHEAD], vs[half][c]
        wait_near(half, bu, bv)
        send(half, bu, bv, ("sib2", c), sib, sib_recv)

    def from_far(half, c):
        bu, bv = us[half][FAR], vs[half][c]
        wait_near(half, bu, bv)
        send(half, bu, bv, ("sib3", c), sib, sib_recv)

    def chunk(half, places, first=False):
        blocks = [(us[half][a], vs[half][b]) for a, b in places]
        for bu, bv in blocks:
            wait_sib(half, bu, bv)
        attend(half, blocks, first)

    line = [(OWN, c) for c in (OWN, NEXT, PREV, FAR)]
    close = [(a, c) for a in (BACK, AHEAD) for c in (OWN, NEXT)]
    wide_off = [(a, c) for a in (BACK, AHEAD) for c in (PREV, FAR)]
    last = [(FAR, c) for c in (OWN, NEXT, PREV, FAR)]

    both(line_sends)
    for half in range(2):
        spread(half, uv[half][1], OWN)
    both(line_near)
    both(from_back, OWN)
    both(from_ahead, OWN)
    both(line_far)
    chunk(0, line, True)
    both(from_back, NEXT)
    both(from_ahead, NEXT)
    chunk(1, line, True)
    both(from_back, PREV)
    both(from_ahead, PREV)
    both(from_far, OWN)
    chunk(0, close)
    both(from_back, FAR)
    both(from_far, NEXT)
    chunk(1, close)
    both(from_ahead, FAR)
    both(from_far, PREV)
    chunk(0, wide_off)
    both(from_far, FAR)
    chunk(1, wide_off)
    chunk(0, last)
    chunk(1, last)

    for pair in range(PAIRS):
        share = 1.0 / acc[pair, 128:129, :]
        even = acc[pair, :64, :ROWS] * share[:, :ROWS]
        odd = acc[pair, 64:128, ROWS:] * share[:, ROWS:]
        mixed[:, pair * 128 : (pair + 1) * 128] = jnp.concatenate([even, odd], axis=0).T.astype(BF16)

    loads[3].wait()
    loads[4].wait()
    projected = jnp.dot(mixed[...], wo[...], preferred_element_type=F32)
    hidden = (feat[...].astype(F32) + projected).astype(BF16)
    wide = hidden.astype(F32)
    feat[...] = hidden
    normed = (wide * lax.rsqrt(jnp.mean(wide * wide, axis=-1, keepdims=True) + 1e-06)).astype(BF16)
    nrm[...] = normed.reshape(2, LON, D)

    up = pltpu.make_async_remote_copy(
        src_ref=nrm.at[0], dst_ref=halo.at[1], send_sem=halo_send.at[0],
        recv_sem=halo_recv.at[1], device_id=prv_id, device_id_type=MESH,
    )
    down = pltpu.make_async_remote_copy(
        src_ref=nrm.at[1], dst_ref=halo.at[0], send_sem=halo_send.at[1],
        recv_sem=halo_recv.at[0], device_id=nxt_id, device_id_type=MESH,
    )
    up.start()
    down.start()

    def neighbours(field):
        wide_field = field.astype(F32)
        left = pltpu.roll(wide_field, 1, 0).astype(BF16)
        right = pltpu.roll(wide_field, LON - 1, 0).astype(BF16)
        return jnp.concatenate([left, field, right], axis=1)

    loads[5].wait()
    pair_rows = jnp.concatenate([neighbours(nrm[0]), neighbours(nrm[1])], axis=1)
    top_row = jnp.dot(pair_rows, wc[1:3].reshape(6 * D, D), preferred_element_type=F32)
    low_row = jnp.dot(pair_rows, wc[0:2].reshape(6 * D, D), preferred_element_type=F32)

    down.wait_recv()
    above = jnp.where(me > 0, halo[0].astype(F32), 0.0).astype(BF16)
    top_row = top_row + jnp.dot(
        neighbours(above), wc[0].reshape(3 * D, D), preferred_element_type=F32
    )
    out_ref[:LON] = (feat[:LON].astype(F32) + top_row).astype(BF16)
    up.wait_recv()
    below = jnp.where(me < 255, halo[1].astype(F32), 0.0).astype(BF16)
    low_row = low_row + jnp.dot(
        neighbours(below), wc[2].reshape(3 * D, D), preferred_element_type=F32
    )
    out_ref[LON:] = (feat[LON:].astype(F32) + low_row).astype(BF16)

    for dz in range(1, NZ):
        for c in range(2):
            z_copy(dz, c).wait_send()
    sib_copy.wait_send()
    for copy in sent:
        copy.wait_send()
    up.wait_send()
    down.wait_send()


def on_device(grid_feat, queries, obs_keys, obs_values, block_mask, obs_valid, out_weight, conv_weight):
    hbm = pl.BlockSpec(memory_space=pltpu.HBM)
    return pl.pallas_call(
        kernel,
        out_shape=jax.ShapeDtypeStruct((ROWS, D), BF16),
        in_specs=[hbm] * 8,
        out_specs=pl.BlockSpec(memory_space=pltpu.VMEM),
        scratch_shapes=[
            pltpu.SMEM((2, 16), jnp.int32),
            pltpu.SMEM((16,), jnp.int32),
            pltpu.VMEM((2, 8, D), BF16),
            pltpu.VMEM((NZ, 2, 8, D), BF16),
            pltpu.VMEM((2, 2, 4, 4, 128, 256), BF16),
            pltpu.VMEM((NX, NY, 128, 128), BF16),
            pltpu.VMEM((ROWS, D), BF16),
            pltpu.VMEM((PAIRS, 256, 512), BF16),
            pltpu.VMEM((ROWS, D), BF16),
            pltpu.VMEM((D, D), BF16),
            pltpu.VMEM((3, 3, D, D), BF16),
            pltpu.VMEM((PAIRS, 144, 512), F32),
            pltpu.VMEM((PAIRS, 8, 512), F32),
            pltpu.VMEM((ROWS, D), BF16),
            pltpu.VMEM((2, LON, D), BF16),
            pltpu.VMEM((2, LON, D), BF16),
            pltpu.SemaphoreType.DMA((8,)),
            pltpu.SemaphoreType.DMA((NZ, 2)),
            pltpu.SemaphoreType.DMA((NZ, 2)),
            pltpu.SemaphoreType.DMA((64,)),
            pltpu.SemaphoreType.DMA((2, 4, 4)),
            pltpu.SemaphoreType.DMA((2, 4, 4)),
            pltpu.SemaphoreType.DMA((2,)),
            pltpu.SemaphoreType.DMA((2,)),
        ],
        compiler_params=pltpu.CompilerParams(
            collective_id=0, has_side_effects=True, vmem_limit_bytes=58 * 1024 * 1024
        ),
    )(block_mask, obs_valid, grid_feat, queries, obs_keys, obs_values, out_weight, conv_weight)


def solution(mesh):
    rows = P(("blk", "tile"), None)
    return jax.shard_map(
        on_device,
        mesh=mesh,
        in_specs=(rows, rows, rows, rows, rows, P(), P(), P()),
        out_specs=rows,
        check_vma=False,
    )
```

```python
import jax
import jax.numpy as jnp
from jax import lax
from jax.experimental import pallas as pl
from jax.experimental.pallas import tpu as pltpu
from jax.sharding import PartitionSpec as P

MESH = pl.DeviceIdType.MESH
NX, NY, NZ = 4, 4, 8
LON = 128
D = 512
ROWS = 256
PAIRS = 4
NEG = -1e30
F32 = jnp.float32
BF16 = jnp.bfloat16


def ring(i, n):
    return lax.rem(i + n, n)


def device(x, y, z, core):
    return (x * 2 + y // 2, z * 4 + lax.rem(y, 2) * 2 + core)


def kernel(
    mask_hbm, valid_hbm, feat_hbm, q_hbm, k_hbm, v_hbm, wo_hbm, wc_hbm, out_ref,
    mask_ref, valid_ref, own, stage, kv, bias, q_ref, qt, feat, wo, wc, acc, top, mixed, nrm, halo,
    load_sem, z_send, z_recv, send_sem, near_recv, sib_recv, halo_send, halo_recv,
):
    blk = lax.axis_index("blk")
    tile = lax.axis_index("tile")
    x = blk // 2
    y = lax.rem(blk, 2) * 2 + lax.rem(tile // 2, 2)
    z = tile // 4
    core = lax.rem(tile, 2)
    sib = device(x, y, z, 1 - core)
    me = blk * 32 + tile
    nxt = lax.rem(me + 1, 256)
    prv = lax.rem(me + 255, 256)
    nxt_id = (nxt // 32, lax.rem(nxt, 32))
    prv_id = (prv // 32, lax.rem(prv, 32))
    side = 1 - 2 * core

    loads = [
        pltpu.make_async_copy(k_hbm, own.at[0], load_sem.at[0]),
        pltpu.make_async_copy(v_hbm, own.at[1], load_sem.at[1]),
        pltpu.make_async_copy(q_hbm, q_ref, load_sem.at[2]),
        pltpu.make_async_copy(feat_hbm, feat, load_sem.at[3]),
        pltpu.make_async_copy(wo_hbm, wo, load_sem.at[4]),
        pltpu.make_async_copy(wc_hbm, wc, load_sem.at[5]),
        pltpu.make_async_copy(mask_hbm, mask_ref, load_sem.at[6]),
        pltpu.make_async_copy(valid_hbm, valid_ref, load_sem.at[7]),
    ]
    loads[0].start()
    loads[1].start()

    barrier = pltpu.get_barrier_semaphore()

    def greet(dev):
        pl.semaphore_signal(barrier, inc=1, device_id=dev, device_id_type=MESH)

    greet(sib)
    for dz in range(1, NZ):
        for c in range(2):
            greet(device(x, y, ring(z + dz, NZ), c))
    for d in (1, 2, 3):
        greet(device(ring(x + d, NX), y, z, core))
        greet(device(x, ring(y + d, NY), z, core))
    greet(nxt_id)
    greet(prv_id)
    for load in loads[2:]:
        load.start()
    loads[0].wait()
    loads[1].wait()
    pl.semaphore_wait(barrier, 23)

    def z_copy(dz, c):
        return pltpu.make_async_remote_copy(
            src_ref=own.at[c],
            dst_ref=stage.at[z, core],
            send_sem=z_send.at[dz, c],
            recv_sem=z_recv.at[z, core],
            device_id=device(x, y, ring(z + dz, NZ), c),
            device_id_type=MESH,
        )

    for dz in (4, 3, 5, 2, 6, 1, 7):
        for c in range(2):
            z_copy(dz, c).start()
    sib_copy = pltpu.make_async_remote_copy(
        src_ref=own.at[1 - core],
        dst_ref=stage.at[z, core],
        send_sem=z_send.at[0, 0],
        recv_sem=z_recv.at[z, core],
        device_id=sib,
        device_id_type=MESH,
    )
    sib_copy.start()
    stage[z, core] = own[core]

    loads[2].wait()
    feat_row = lax.broadcasted_iota(jnp.int32, (128, ROWS), 0)
    query_col = lax.broadcasted_iota(jnp.int32, (128, ROWS), 1)
    onehot = jnp.where(feat_row == query_col // LON, 1.0, 0.0).astype(BF16)
    for p in range(PAIRS):
        part = (q_ref[:, p * 128 : (p + 1) * 128].astype(F32) * 0.125).T
        qt[p, :128, :ROWS] = jnp.where(feat_row < 64, part, 0.0).astype(BF16)
        qt[p, :128, ROWS:] = jnp.where(feat_row >= 64, part, 0.0).astype(BF16)
        qt[p, 128:, :ROWS] = onehot
        qt[p, 128:, ROWS:] = onehot

    key = lax.broadcasted_iota(jnp.int32, (128, 128), 0)
    col = lax.broadcasted_iota(jnp.int32, (128, 128), 1)
    low = key < 64

    loads[6].wait()
    loads[7].wait()

    def mask_block(i, carry):
        kx, ky = i // NY, lax.rem(i, NY)
        b0 = kx * 4 + (ky // 2) * 2
        b1 = b0 + 1
        place = ((key >> 4) & 3) * 32 + (key & 15) + lax.rem(ky, 2) * 16
        limit = jnp.where(low, valid_ref[b0], valid_ref[b1])
        first = jnp.where(low, mask_ref[0, b0], mask_ref[0, b1])
        second = jnp.where(low, mask_ref[1, b0], mask_ref[1, b1])
        wanted = jnp.where(col == 0, first, second)
        live = jnp.where(place < limit, wanted, 0)
        live = jnp.where(col < 2, live, 1)
        bias[kx, ky] = jnp.where(live > 0, 0.0, NEG).astype(BF16)
        return carry

    lax.fori_loop(0, NX * NY, mask_block, 0)

    for dz in range(NZ):
        for c in range(2):
            src_z = ring(z + dz, NZ)

            def arrival(cc):
                return pltpu.make_async_remote_copy(
                    src_ref=own.at[0],
                    dst_ref=stage.at[src_z, cc],
                    send_sem=z_send.at[0, 1],
                    recv_sem=z_recv.at[src_z, cc],
                    device_id=sib,
                    device_id_type=MESH,
                )

            if dz == 0:
                if c == 0:
                    arrival(1 - core).wait_recv()
            else:
                arrival(c).wait_recv()
    plain = stage[...].astype(F32).reshape(128, D)
    turned = jnp.concatenate([plain[:, p * 128 : (p + 1) * 128].T for p in range(PAIRS)], axis=1)
    block = jnp.where(core == 0, plain, turned).astype(BF16)

    uv = ((x, y), (y, x))
    for half in range(2):
        u, v = uv[half]
        kv[core, half, u, v] = block[:, half * 256 : (half + 1) * 256]

    def dev_of(half, u, v, c):
        return device(u, v, z, c) if half == 0 else device(v, u, z, c)

    slots = {}

    def copy_block(half, bu, bv, name, target, recv):
        slot = slots.setdefault((half, name), len(slots))
        return pltpu.make_async_remote_copy(
            src_ref=kv.at[core, half, bu, bv],
            dst_ref=kv.at[core, half, bu, bv],
            send_sem=send_sem.at[slot],
            recv_sem=recv.at[half, bu, bv],
            device_id=target,
            device_id_type=MESH,
        )

    sent = []

    def send(half, bu, bv, name, target, recv=None):
        copy = copy_block(half, bu, bv, name, target, near_recv if recv is None else recv)
        copy.start()
        sent.append(copy)

    def wait_near(half, bu, bv):
        pltpu.make_async_remote_copy(
            src_ref=kv.at[core, half, bu, bv],
            dst_ref=kv.at[core, half, bu, bv],
            send_sem=send_sem.at[0],
            recv_sem=near_recv.at[half, bu, bv],
            device_id=sib,
            device_id_type=MESH,
        ).wait_recv()

    def wait_sib(half, bu, bv):
        pltpu.make_async_remote_copy(
            src_ref=kv.at[1 - core, half, bu, bv],
            dst_ref=kv.at[1 - core, half, bu, bv],
            send_sem=send_sem.at[0],
            recv_sem=sib_recv.at[half, bu, bv],
            device_id=sib,
            device_id_type=MESH,
        ).wait_recv()

    def spread(half, bv, tag):
        u, v = uv[half]
        for d in (1, 3):
            send(half, u, bv, ("u", tag, d), dev_of(half, ring(u + d, 4), v, core))
        send(half, u, bv, ("sib", tag), sib, sib_recv)


    def attend(half, blocks, first):
        ones = jnp.ones((16, 128 * len(blocks)), BF16)
        for p in range(2):
            pair = half * 2 + p
            cols = slice(p * 128, (p + 1) * 128)
            keys = [kv[0, half, bu, bv, :, cols] for bu, bv in blocks]
            values = [kv[1, half, bu, bv, :, cols] for bu, bv in blocks]
            shut = [bias[bu, bv] if half == 0 else bias[bv, bu] for bu, bv in blocks]
            scores = jnp.dot(
                jnp.concatenate(
                    [jnp.concatenate(keys, axis=0), jnp.concatenate(shut, axis=0)], axis=1
                ),
                qt[pair],
                preferred_element_type=F32,
            )
            peak = jnp.max(scores, axis=0, keepdims=True)
            if first:
                new_top = jnp.broadcast_to(peak, (8, 512))
            else:
                old_top = top[pair]
                new_top = jnp.maximum(old_top, peak)
            weights = jnp.exp(scores - new_top[:1]).astype(BF16)
            part = jnp.dot(
                jnp.concatenate([jnp.concatenate(values, axis=1), ones], axis=0),
                weights,
                preferred_element_type=F32,
            )
            if first:
                acc[pair] = part
            else:
                factor = jnp.exp(old_top - new_top)
                acc[pair] = acc[pair] * factor[:1] + part
            top[pair] = new_top

    us = []
    vs = []
    for half in range(2):
        u, v = uv[half]
        us.append((u, ring(u - side, 4), ring(u + side, 4), ring(u + 2, 4)))
        vs.append((v, ring(v + 1, 4), ring(v - 1, 4), ring(v + 2, 4)))
    OWN, NEXT, PREV, FAR = 0, 1, 2, 3
    BACK, AHEAD = 1, 2

    def both(step, *args):
        for half in range(2):
            step(half, *args)

    def line_sends(half):
        u, v = uv[half]
        for d in (1, 3, 2):
            send(half, u, v, ("v", d), dev_of(half, u, ring(v + d, 4), core))

    def line_near(half):
        u, v = uv[half]
        wait_near(half, u, vs[half][NEXT])
        spread(half, vs[half][NEXT], NEXT)
        wait_near(half, u, vs[half][PREV])
        spread(half, vs[half][PREV], PREV)

    def line_far(half):
        wait_near(half, uv[half][0], vs[half][FAR])
        spread(half, vs[half][FAR], FAR)

    def from_back(half, c):
        bu, bv = us[half][BACK], vs[half][c]
        wait_near(half, bu, bv)
        send(half, bu, bv, ("relay", c), dev_of(half, us[half][AHEAD], uv[half][1], core))
        send(half, bu, bv, ("sib1", c), sib, sib_recv)

    def from_ahead(half, c):
        bu, bv = us[half][AHEAD], vs[half][c]
        wait_near(half, bu, bv)
        send(half, bu, bv, ("sib2", c), sib, sib_recv)

    def from_far(half, c):
        bu, bv = us[half][FAR], vs[half][c]
        wait_near(half, bu, bv)
        send(half, bu, bv, ("sib3", c), sib, sib_recv)

    def chunk(half, places, first=False):
        blocks = [(us[half][a], vs[half][b]) for a, b in places]
        for bu, bv in blocks:
            wait_sib(half, bu, bv)
        attend(half, blocks, first)

    line = [(OWN, c) for c in (OWN, NEXT, PREV, FAR)]
    close = [(a, c) for a in (BACK, AHEAD) for c in (OWN, NEXT)]
    wide_off = [(a, c) for a in (BACK, AHEAD) for c in (PREV, FAR)]
    early = [(FAR, c) for c in (OWN, NEXT)]
    last = [(FAR, c) for c in (PREV, FAR)]

    both(line_sends)
    for half in range(2):
        spread(half, uv[half][1], OWN)
    both(line_near)
    both(from_back, OWN)
    both(from_ahead, OWN)
    both(line_far)
    chunk(0, line, True)
    both(from_back, NEXT)
    both(from_ahead, NEXT)
    chunk(1, line, True)
    both(from_back, PREV)
    both(from_ahead, PREV)
    both(from_far, OWN)
    chunk(0, close)
    both(from_back, FAR)
    both(from_ahead, FAR)
    chunk(1, close)
    both(from_far, NEXT)
    chunk(0, wide_off)
    chunk(1, wide_off)
    both(from_far, PREV)
    both(from_far, FAR)
    chunk(0, early)
    chunk(1, early)
    chunk(0, last)
    chunk(1, last)

    for pair in range(PAIRS):
        share = 1.0 / acc[pair, 128:129, :]
        even = acc[pair, :64, :ROWS] * share[:, :ROWS]
        odd = acc[pair, 64:128, ROWS:] * share[:, ROWS:]
        mixed[:, pair * 128 : (pair + 1) * 128] = jnp.concatenate([even, odd], axis=0).T.astype(BF16)

    loads[3].wait()
    loads[4].wait()
    projected = jnp.dot(mixed[...], wo[...], preferred_element_type=F32)
    hidden = (feat[...].astype(F32) + projected).astype(BF16)
    wide = hidden.astype(F32)
    feat[...] = hidden
    normed = (wide * lax.rsqrt(jnp.mean(wide * wide, axis=-1, keepdims=True) + 1e-06)).astype(BF16)
    nrm[...] = normed.reshape(2, LON, D)

    up = pltpu.make_async_remote_copy(
        src_ref=nrm.at[0], dst_ref=halo.at[1], send_sem=halo_send.at[0],
        recv_sem=halo_recv.at[1], device_id=prv_id, device_id_type=MESH,
    )
    down = pltpu.make_async_remote_copy(
        src_ref=nrm.at[1], dst_ref=halo.at[0], send_sem=halo_send.at[1],
        recv_sem=halo_recv.at[0], device_id=nxt_id, device_id_type=MESH,
    )
    up.start()
    down.start()

    def neighbours(field):
        wide_field = field.astype(F32)
        left = pltpu.roll(wide_field, 1, 0).astype(BF16)
        right = pltpu.roll(wide_field, LON - 1, 0).astype(BF16)
        return jnp.concatenate([left, field, right], axis=1)

    loads[5].wait()
    pair_rows = jnp.concatenate([neighbours(nrm[0]), neighbours(nrm[1])], axis=1)
    top_row = jnp.dot(pair_rows, wc[1:3].reshape(6 * D, D), preferred_element_type=F32)
    low_row = jnp.dot(pair_rows, wc[0:2].reshape(6 * D, D), preferred_element_type=F32)

    down.wait_recv()
    above = jnp.where(me > 0, halo[0].astype(F32), 0.0).astype(BF16)
    top_row = top_row + jnp.dot(
        neighbours(above), wc[0].reshape(3 * D, D), preferred_element_type=F32
    )
    out_ref[:LON] = (feat[:LON].astype(F32) + top_row).astype(BF16)
    up.wait_recv()
    below = jnp.where(me < 255, halo[1].astype(F32), 0.0).astype(BF16)
    low_row = low_row + jnp.dot(
        neighbours(below), wc[2].reshape(3 * D, D), preferred_element_type=F32
    )
    out_ref[LON:] = (feat[LON:].astype(F32) + low_row).astype(BF16)

    for dz in range(1, NZ):
        for c in range(2):
            z_copy(dz, c).wait_send()
    sib_copy.wait_send()
    for copy in sent:
        copy.wait_send()
    up.wait_send()
    down.wait_send()


def on_device(grid_feat, queries, obs_keys, obs_values, block_mask, obs_valid, out_weight, conv_weight):
    hbm = pl.BlockSpec(memory_space=pltpu.HBM)
    return pl.pallas_call(
        kernel,
        out_shape=jax.ShapeDtypeStruct((ROWS, D), BF16),
        in_specs=[hbm] * 8,
        out_specs=pl.BlockSpec(memory_space=pltpu.VMEM),
        scratch_shapes=[
            pltpu.SMEM((2, 16), jnp.int32),
            pltpu.SMEM((16,), jnp.int32),
            pltpu.VMEM((2, 8, D), BF16),
            pltpu.VMEM((NZ, 2, 8, D), BF16),
            pltpu.VMEM((2, 2, 4, 4, 128, 256), BF16),
            pltpu.VMEM((NX, NY, 128, 128), BF16),
            pltpu.VMEM((ROWS, D), BF16),
            pltpu.VMEM((PAIRS, 256, 512), BF16),
            pltpu.VMEM((ROWS, D), BF16),
            pltpu.VMEM((D, D), BF16),
            pltpu.VMEM((3, 3, D, D), BF16),
            pltpu.VMEM((PAIRS, 144, 512), F32),
            pltpu.VMEM((PAIRS, 8, 512), F32),
            pltpu.VMEM((ROWS, D), BF16),
            pltpu.VMEM((2, LON, D), BF16),
            pltpu.VMEM((2, LON, D), BF16),
            pltpu.SemaphoreType.DMA((8,)),
            pltpu.SemaphoreType.DMA((NZ, 2)),
            pltpu.SemaphoreType.DMA((NZ, 2)),
            pltpu.SemaphoreType.DMA((64,)),
            pltpu.SemaphoreType.DMA((2, 4, 4)),
            pltpu.SemaphoreType.DMA((2, 4, 4)),
            pltpu.SemaphoreType.DMA((2,)),
            pltpu.SemaphoreType.DMA((2,)),
        ],
        compiler_params=pltpu.CompilerParams(
            collective_id=0, has_side_effects=True, vmem_limit_bytes=58 * 1024 * 1024
        ),
    )(block_mask, obs_valid, grid_feat, queries, obs_keys, obs_values, out_weight, conv_weight)


def solution(mesh):
    rows = P(("blk", "tile"), None)
    return jax.shard_map(
        on_device,
        mesh=mesh,
        in_specs=(rows, rows, rows, rows, rows, P(), P(), P()),
        out_specs=rows,
        check_vma=False,
    )
```

```python
import jax
import jax.numpy as jnp
from jax import lax
from jax.experimental import pallas as pl
from jax.experimental.pallas import tpu as pltpu
from jax.sharding import PartitionSpec as P

MESH = pl.DeviceIdType.MESH
NX, NY, NZ = 4, 4, 8
LON = 128
D = 512
ROWS = 256
PAIRS = 4
NEG = -1e30
F32 = jnp.float32
BF16 = jnp.bfloat16


def ring(i, n):
    return lax.rem(i + n, n)


def device(x, y, z, core):
    return (x * 2 + y // 2, z * 4 + lax.rem(y, 2) * 2 + core)


def kernel(
    mask_hbm, valid_hbm, feat_hbm, q_hbm, k_hbm, v_hbm, wo_hbm, wc_hbm, out_hbm,
    mask_ref, valid_ref, own, stage, kv, bias, q_ref, qt, feat, wo, wc, acc, top, mixed, nrm, halo,
    load_sem, z_send, z_recv, send_sem, near_recv, sib_recv, halo_send, halo_recv, out_ref, out_sem,
):
    blk = lax.axis_index("blk")
    tile = lax.axis_index("tile")
    x = blk // 2
    y = lax.rem(blk, 2) * 2 + lax.rem(tile // 2, 2)
    z = tile // 4
    core = lax.rem(tile, 2)
    sib = device(x, y, z, 1 - core)
    me = blk * 32 + tile
    nxt = lax.rem(me + 1, 256)
    prv = lax.rem(me + 255, 256)
    nxt_id = (nxt // 32, lax.rem(nxt, 32))
    prv_id = (prv // 32, lax.rem(prv, 32))
    side = 1 - 2 * core

    loads = [
        pltpu.make_async_copy(k_hbm, own.at[0], load_sem.at[0]),
        pltpu.make_async_copy(v_hbm, own.at[1], load_sem.at[1]),
        pltpu.make_async_copy(q_hbm, q_ref, load_sem.at[2]),
        pltpu.make_async_copy(feat_hbm, feat, load_sem.at[3]),
        pltpu.make_async_copy(wo_hbm, wo, load_sem.at[4]),
        pltpu.make_async_copy(wc_hbm, wc, load_sem.at[5]),
        pltpu.make_async_copy(mask_hbm, mask_ref, load_sem.at[6]),
        pltpu.make_async_copy(valid_hbm, valid_ref, load_sem.at[7]),
    ]
    loads[0].start()
    loads[1].start()

    barrier = pltpu.get_barrier_semaphore()

    def greet(dev):
        pl.semaphore_signal(barrier, inc=1, device_id=dev, device_id_type=MESH)

    greet(sib)
    for dz in range(1, NZ):
        for c in range(2):
            greet(device(x, y, ring(z + dz, NZ), c))
    for d in (1, 2, 3):
        greet(device(ring(x + d, NX), y, z, core))
        greet(device(x, ring(y + d, NY), z, core))
    greet(nxt_id)
    greet(prv_id)
    for load in loads[2:]:
        load.start()
    loads[0].wait()
    loads[1].wait()
    pl.semaphore_wait(barrier, 23)

    def z_copy(dz, c):
        return pltpu.make_async_remote_copy(
            src_ref=own.at[c],
            dst_ref=stage.at[z, core],
            send_sem=z_send.at[dz, c],
            recv_sem=z_recv.at[z, core],
            device_id=device(x, y, ring(z + dz, NZ), c),
            device_id_type=MESH,
        )

    for dz in (4, 3, 5, 2, 6, 1, 7):
        for c in range(2):
            z_copy(dz, c).start()
    sib_copy = pltpu.make_async_remote_copy(
        src_ref=own.at[1 - core],
        dst_ref=stage.at[z, core],
        send_sem=z_send.at[0, 0],
        recv_sem=z_recv.at[z, core],
        device_id=sib,
        device_id_type=MESH,
    )
    sib_copy.start()
    stage[z, core] = own[core]

    loads[2].wait()
    feat_row = lax.broadcasted_iota(jnp.int32, (128, ROWS), 0)
    query_col = lax.broadcasted_iota(jnp.int32, (128, ROWS), 1)
    onehot = jnp.where(feat_row == query_col // LON, 1.0, 0.0).astype(BF16)
    for p in range(PAIRS):
        part = (q_ref[:, p * 128 : (p + 1) * 128].astype(F32) * 0.125).T
        qt[p, :128, :ROWS] = jnp.where(feat_row < 64, part, 0.0).astype(BF16)
        qt[p, :128, ROWS:] = jnp.where(feat_row >= 64, part, 0.0).astype(BF16)
        qt[p, 128:, :ROWS] = onehot
        qt[p, 128:, ROWS:] = onehot

    key = lax.broadcasted_iota(jnp.int32, (128, 128), 0)
    col = lax.broadcasted_iota(jnp.int32, (128, 128), 1)
    low = key < 64

    loads[6].wait()
    loads[7].wait()

    def mask_block(i, carry):
        kx, ky = i // NY, lax.rem(i, NY)
        b0 = kx * 4 + (ky // 2) * 2
        b1 = b0 + 1
        place = ((key >> 4) & 3) * 32 + (key & 15) + lax.rem(ky, 2) * 16
        limit = jnp.where(low, valid_ref[b0], valid_ref[b1])
        first = jnp.where(low, mask_ref[0, b0], mask_ref[0, b1])
        second = jnp.where(low, mask_ref[1, b0], mask_ref[1, b1])
        wanted = jnp.where(col == 0, first, second)
        live = jnp.where(place < limit, wanted, 0)
        live = jnp.where(col < 2, live, 1)
        bias[kx, ky] = jnp.where(live > 0, 0.0, NEG).astype(BF16)
        return carry

    lax.fori_loop(0, NX * NY, mask_block, 0)

    for dz in range(NZ):
        for c in range(2):
            src_z = ring(z + dz, NZ)

            def arrival(cc):
                return pltpu.make_async_remote_copy(
                    src_ref=own.at[0],
                    dst_ref=stage.at[src_z, cc],
                    send_sem=z_send.at[0, 1],
                    recv_sem=z_recv.at[src_z, cc],
                    device_id=sib,
                    device_id_type=MESH,
                )

            if dz == 0:
                if c == 0:
                    arrival(1 - core).wait_recv()
            else:
                arrival(c).wait_recv()
    plain = stage[...].astype(F32).reshape(128, D)
    turned = jnp.concatenate([plain[:, p * 128 : (p + 1) * 128].T for p in range(PAIRS)], axis=1)
    block = jnp.where(core == 0, plain, turned).astype(BF16)

    uv = ((x, y), (y, x))
    for half in range(2):
        u, v = uv[half]
        kv[core, half, u, v] = block[:, half * 256 : (half + 1) * 256]

    def dev_of(half, u, v, c):
        return device(u, v, z, c) if half == 0 else device(v, u, z, c)

    slots = {}

    def copy_block(half, bu, bv, name, target, recv):
        slot = slots.setdefault((half, name), len(slots))
        return pltpu.make_async_remote_copy(
            src_ref=kv.at[core, half, bu, bv],
            dst_ref=kv.at[core, half, bu, bv],
            send_sem=send_sem.at[slot],
            recv_sem=recv.at[half, bu, bv],
            device_id=target,
            device_id_type=MESH,
        )

    sent = []

    def send(half, bu, bv, name, target, recv=None):
        copy = copy_block(half, bu, bv, name, target, near_recv if recv is None else recv)
        copy.start()
        sent.append(copy)

    def wait_near(half, bu, bv):
        pltpu.make_async_remote_copy(
            src_ref=kv.at[core, half, bu, bv],
            dst_ref=kv.at[core, half, bu, bv],
            send_sem=send_sem.at[0],
            recv_sem=near_recv.at[half, bu, bv],
            device_id=sib,
            device_id_type=MESH,
        ).wait_recv()

    def wait_sib(half, bu, bv):
        pltpu.make_async_remote_copy(
            src_ref=kv.at[1 - core, half, bu, bv],
            dst_ref=kv.at[1 - core, half, bu, bv],
            send_sem=send_sem.at[0],
            recv_sem=sib_recv.at[half, bu, bv],
            device_id=sib,
            device_id_type=MESH,
        ).wait_recv()

    def spread(half, bv, tag):
        u, v = uv[half]
        for d in (1, 3):
            send(half, u, bv, ("u", tag, d), dev_of(half, ring(u + d, 4), v, core))
        send(half, u, bv, ("sib", tag), sib, sib_recv)


    def attend(half, blocks, first):
        ones = jnp.ones((16, 128 * len(blocks)), BF16)
        for p in range(2):
            pair = half * 2 + p
            cols = slice(p * 128, (p + 1) * 128)
            keys = [kv[0, half, bu, bv, :, cols] for bu, bv in blocks]
            values = [kv[1, half, bu, bv, :, cols] for bu, bv in blocks]
            shut = [bias[bu, bv] if half == 0 else bias[bv, bu] for bu, bv in blocks]
            scores = jnp.dot(
                jnp.concatenate(
                    [jnp.concatenate(keys, axis=0), jnp.concatenate(shut, axis=0)], axis=1
                ),
                qt[pair],
                preferred_element_type=F32,
            )
            peak = jnp.max(scores, axis=0, keepdims=True)
            if first:
                new_top = jnp.broadcast_to(peak, (8, 512))
            else:
                old_top = top[pair]
                new_top = jnp.maximum(old_top, peak)
            weights = jnp.exp(scores - new_top[:1]).astype(BF16)
            part = jnp.dot(
                jnp.concatenate([jnp.concatenate(values, axis=1), ones], axis=0),
                weights,
                preferred_element_type=F32,
            )
            if first:
                acc[pair] = part
            else:
                factor = jnp.exp(old_top - new_top)
                acc[pair] = acc[pair] * factor[:1] + part
            top[pair] = new_top

    us = []
    vs = []
    for half in range(2):
        u, v = uv[half]
        us.append((u, ring(u - side, 4), ring(u + side, 4), ring(u + 2, 4)))
        vs.append((v, ring(v + 1, 4), ring(v - 1, 4), ring(v + 2, 4)))
    OWN, NEXT, PREV, FAR = 0, 1, 2, 3
    BACK, AHEAD = 1, 2

    def both(step, *args):
        for half in range(2):
            step(half, *args)

    def line_sends(half):
        u, v = uv[half]
        for d in (1, 3):
            send(half, u, v, ("v", d), dev_of(half, u, ring(v + d, 4), core))

    def line_near(half):
        u, v = uv[half]
        wait_near(half, u, vs[half][NEXT])
        spread(half, vs[half][NEXT], NEXT)
        wait_near(half, u, vs[half][PREV])
        spread(half, vs[half][PREV], PREV)

    def line_far(half):
        wait_near(half, uv[half][0], vs[half][FAR])
        spread(half, vs[half][FAR], FAR)

    def from_back(half, c):
        bu, bv = us[half][BACK], vs[half][c]
        wait_near(half, bu, bv)
        send(half, bu, bv, ("relay", c), dev_of(half, us[half][AHEAD], uv[half][1], core))
        send(half, bu, bv, ("sib1", c), sib, sib_recv)

    def from_ahead(half, c):
        bu, bv = us[half][AHEAD], vs[half][c]
        wait_near(half, bu, bv)
        send(half, bu, bv, ("sib2", c), sib, sib_recv)

    def from_far(half, c):
        bu, bv = us[half][FAR], vs[half][c]
        wait_near(half, bu, bv)
        send(half, bu, bv, ("sib3", c), sib, sib_recv)

    def chunk(half, places, first=False):
        blocks = [(us[half][a], vs[half][b]) for a, b in places]
        for bu, bv in blocks:
            wait_sib(half, bu, bv)
        attend(half, blocks, first)

    line = [(OWN, c) for c in (OWN, NEXT, PREV, FAR)]
    close = [(a, c) for a in (BACK, AHEAD) for c in (OWN, NEXT)]
    wide_off = [(a, c) for a in (BACK, AHEAD) for c in (PREV, FAR)]
    early = [(FAR, c) for c in (OWN, NEXT)]
    last = [(FAR, c) for c in (PREV, FAR)]

    both(line_sends)
    for half in range(2):
        spread(half, uv[half][1], OWN)
    for half in range(2):
        u, v = uv[half]
        send(half, u, v, ("v", 2), dev_of(half, u, ring(v + 2, 4), core))
    both(line_near)
    both(from_back, OWN)
    both(from_ahead, OWN)
    both(line_far)
    chunk(0, line, True)
    both(from_back, NEXT)
    both(from_ahead, NEXT)
    chunk(1, line, True)
    both(from_back, PREV)
    both(from_ahead, PREV)
    both(from_far, OWN)
    chunk(0, close)
    both(from_back, FAR)
    both(from_ahead, FAR)
    chunk(1, close)
    both(from_far, NEXT)
    chunk(0, wide_off)
    chunk(1, wide_off)
    both(from_far, PREV)
    both(from_far, FAR)
    chunk(0, early)
    chunk(1, early)
    chunk(0, last)
    chunk(1, last)

    for pair in range(PAIRS):
        share = 1.0 / acc[pair, 128:129, :]
        even = acc[pair, :64, :ROWS] * share[:, :ROWS]
        odd = acc[pair, 64:128, ROWS:] * share[:, ROWS:]
        mixed[:, pair * 128 : (pair + 1) * 128] = jnp.concatenate([even, odd], axis=0).T.astype(BF16)

    loads[3].wait()
    loads[4].wait()
    projected = jnp.dot(mixed[...], wo[...], preferred_element_type=F32)
    hidden = (feat[...].astype(F32) + projected).astype(BF16)
    wide = hidden.astype(F32)
    feat[...] = hidden
    normed = (wide * lax.rsqrt(jnp.mean(wide * wide, axis=-1, keepdims=True) + 1e-06)).astype(BF16)
    nrm[...] = normed.reshape(2, LON, D)

    up = pltpu.make_async_remote_copy(
        src_ref=nrm.at[0], dst_ref=halo.at[1], send_sem=halo_send.at[0],
        recv_sem=halo_recv.at[1], device_id=prv_id, device_id_type=MESH,
    )
    down = pltpu.make_async_remote_copy(
        src_ref=nrm.at[1], dst_ref=halo.at[0], send_sem=halo_send.at[1],
        recv_sem=halo_recv.at[0], device_id=nxt_id, device_id_type=MESH,
    )
    up.start()
    down.start()

    def neighbours(field):
        wide_field = field.astype(F32)
        left = pltpu.roll(wide_field, 1, 0).astype(BF16)
        right = pltpu.roll(wide_field, LON - 1, 0).astype(BF16)
        return jnp.concatenate([left, field, right], axis=1)

    loads[5].wait()
    pair_rows = jnp.concatenate([neighbours(nrm[0]), neighbours(nrm[1])], axis=1)
    top_row = jnp.dot(pair_rows, wc[1:3].reshape(6 * D, D), preferred_element_type=F32)
    low_row = jnp.dot(pair_rows, wc[0:2].reshape(6 * D, D), preferred_element_type=F32)

    down.wait_recv()
    above = jnp.where(me > 0, halo[0].astype(F32), 0.0).astype(BF16)
    top_row = top_row + jnp.dot(
        neighbours(above), wc[0].reshape(3 * D, D), preferred_element_type=F32
    )
    out_ref[:LON] = (feat[:LON].astype(F32) + top_row).astype(BF16)
    upper = pltpu.make_async_copy(out_ref.at[:LON], out_hbm.at[:LON], out_sem.at[0])
    upper.start()
    up.wait_recv()
    below = jnp.where(me < 255, halo[1].astype(F32), 0.0).astype(BF16)
    low_row = low_row + jnp.dot(
        neighbours(below), wc[2].reshape(3 * D, D), preferred_element_type=F32
    )
    out_ref[LON:] = (feat[LON:].astype(F32) + low_row).astype(BF16)
    lower = pltpu.make_async_copy(out_ref.at[LON:], out_hbm.at[LON:], out_sem.at[1])
    lower.start()

    for dz in range(1, NZ):
        for c in range(2):
            z_copy(dz, c).wait_send()
    sib_copy.wait_send()
    for copy in sent:
        copy.wait_send()
    up.wait_send()
    down.wait_send()
    upper.wait()
    lower.wait()


def on_device(grid_feat, queries, obs_keys, obs_values, block_mask, obs_valid, out_weight, conv_weight):
    hbm = pl.BlockSpec(memory_space=pltpu.HBM)
    return pl.pallas_call(
        kernel,
        out_shape=jax.ShapeDtypeStruct((ROWS, D), BF16),
        in_specs=[hbm] * 8,
        out_specs=hbm,
        scratch_shapes=[
            pltpu.SMEM((2, 16), jnp.int32),
            pltpu.SMEM((16,), jnp.int32),
            pltpu.VMEM((2, 8, D), BF16),
            pltpu.VMEM((NZ, 2, 8, D), BF16),
            pltpu.VMEM((2, 2, 4, 4, 128, 256), BF16),
            pltpu.VMEM((NX, NY, 128, 128), BF16),
            pltpu.VMEM((ROWS, D), BF16),
            pltpu.VMEM((PAIRS, 256, 512), BF16),
            pltpu.VMEM((ROWS, D), BF16),
            pltpu.VMEM((D, D), BF16),
            pltpu.VMEM((3, 3, D, D), BF16),
            pltpu.VMEM((PAIRS, 144, 512), F32),
            pltpu.VMEM((PAIRS, 8, 512), F32),
            pltpu.VMEM((ROWS, D), BF16),
            pltpu.VMEM((2, LON, D), BF16),
            pltpu.VMEM((2, LON, D), BF16),
            pltpu.SemaphoreType.DMA((8,)),
            pltpu.SemaphoreType.DMA((NZ, 2)),
            pltpu.SemaphoreType.DMA((NZ, 2)),
            pltpu.SemaphoreType.DMA((64,)),
            pltpu.SemaphoreType.DMA((2, 4, 4)),
            pltpu.SemaphoreType.DMA((2, 4, 4)),
            pltpu.SemaphoreType.DMA((2,)),
            pltpu.SemaphoreType.DMA((2,)),
            pltpu.VMEM((ROWS, D), BF16),
            pltpu.SemaphoreType.DMA((2,)),
        ],
        compiler_params=pltpu.CompilerParams(
            collective_id=0, has_side_effects=True, vmem_limit_bytes=58 * 1024 * 1024
        ),
    )(block_mask, obs_valid, grid_feat, queries, obs_keys, obs_values, out_weight, conv_weight)


def solution(mesh):
    rows = P(("blk", "tile"), None)
    return jax.shard_map(
        on_device,
        mesh=mesh,
        in_specs=(rows, rows, rows, rows, rows, P(), P(), P()),
        out_specs=rows,
        check_vma=False,
    )
```

```python
import jax
import jax.numpy as jnp
from jax import lax
from jax.experimental import pallas as pl
from jax.experimental.pallas import tpu as pltpu
from jax.sharding import PartitionSpec as P

MESH = pl.DeviceIdType.MESH
NX, NY, NZ = 4, 4, 8
LON = 128
D = 512
ROWS = 256
PAIRS = 4
NEG = -1e30
F32 = jnp.float32
BF16 = jnp.bfloat16


def ring(i, n):
    return lax.rem(i + n, n)


def device(x, y, z, core):
    return (x * 2 + y // 2, z * 4 + lax.rem(y, 2) * 2 + core)


def kernel(
    mask_hbm, valid_hbm, feat_hbm, q_hbm, k_hbm, v_hbm, wo_hbm, wc_hbm, out_hbm,
    mask_ref, valid_ref, own, stage, kv, bias, q_ref, qt, feat, wo, wc, acc, top, mixed, nrm, halo,
    load_sem, z_send, z_recv, send_sem, near_recv, sib_recv, halo_send, halo_recv, out_ref, out_sem,
):
    blk = lax.axis_index("blk")
    tile = lax.axis_index("tile")
    x = blk // 2
    y = lax.rem(blk, 2) * 2 + lax.rem(tile // 2, 2)
    z = tile // 4
    core = lax.rem(tile, 2)
    sib = device(x, y, z, 1 - core)
    me = blk * 32 + tile
    nxt = lax.rem(me + 1, 256)
    prv = lax.rem(me + 255, 256)
    nxt_id = (nxt // 32, lax.rem(nxt, 32))
    prv_id = (prv // 32, lax.rem(prv, 32))
    side = 1 - 2 * core

    loads = [
        pltpu.make_async_copy(k_hbm, own.at[0], load_sem.at[0]),
        pltpu.make_async_copy(v_hbm, own.at[1], load_sem.at[1]),
        pltpu.make_async_copy(q_hbm, q_ref, load_sem.at[2]),
        pltpu.make_async_copy(feat_hbm, feat, load_sem.at[3]),
        pltpu.make_async_copy(wo_hbm, wo, load_sem.at[4]),
        pltpu.make_async_copy(wc_hbm, wc, load_sem.at[5]),
        pltpu.make_async_copy(mask_hbm, mask_ref, load_sem.at[6]),
        pltpu.make_async_copy(valid_hbm, valid_ref, load_sem.at[7]),
    ]
    loads[0].start()
    loads[1].start()

    barrier = pltpu.get_barrier_semaphore()

    def greet(dev):
        pl.semaphore_signal(barrier, inc=1, device_id=dev, device_id_type=MESH)

    greet(sib)
    for dz in range(1, NZ):
        for c in range(2):
            greet(device(x, y, ring(z + dz, NZ), c))
    for d in (1, 2, 3):
        greet(device(ring(x + d, NX), y, z, core))
        greet(device(x, ring(y + d, NY), z, core))
    greet(nxt_id)
    greet(prv_id)
    for load in loads[2:]:
        load.start()
    loads[0].wait()
    loads[1].wait()
    pl.semaphore_wait(barrier, 23)

    def z_copy(dz, c):
        return pltpu.make_async_remote_copy(
            src_ref=own.at[c],
            dst_ref=stage.at[z, core],
            send_sem=z_send.at[dz, c],
            recv_sem=z_recv.at[z, core],
            device_id=device(x, y, ring(z + dz, NZ), c),
            device_id_type=MESH,
        )

    for dz in (4, 3, 5, 2, 6, 1, 7):
        for c in range(2):
            z_copy(dz, c).start()
    sib_copy = pltpu.make_async_remote_copy(
        src_ref=own.at[1 - core],
        dst_ref=stage.at[z, core],
        send_sem=z_send.at[0, 0],
        recv_sem=z_recv.at[z, core],
        device_id=sib,
        device_id_type=MESH,
    )
    sib_copy.start()
    stage[z, core] = own[core]

    loads[2].wait()
    feat_row = lax.broadcasted_iota(jnp.int32, (128, ROWS), 0)
    query_col = lax.broadcasted_iota(jnp.int32, (128, ROWS), 1)
    onehot = jnp.where(feat_row == query_col // LON, 1.0, 0.0).astype(BF16)
    for p in range(PAIRS):
        part = (q_ref[:, p * 128 : (p + 1) * 128].astype(F32) * 0.125).T
        qt[p, :128, :ROWS] = jnp.where(feat_row < 64, part, 0.0).astype(BF16)
        qt[p, :128, ROWS:] = jnp.where(feat_row >= 64, part, 0.0).astype(BF16)
        qt[p, 128:, :ROWS] = onehot
        qt[p, 128:, ROWS:] = onehot

    key = lax.broadcasted_iota(jnp.int32, (128, 128), 0)
    col = lax.broadcasted_iota(jnp.int32, (128, 128), 1)
    low = key < 64

    loads[6].wait()
    loads[7].wait()

    def mask_block(i, carry):
        kx, ky = i // NY, lax.rem(i, NY)
        b0 = kx * 4 + (ky // 2) * 2
        b1 = b0 + 1
        place = ((key >> 4) & 3) * 32 + (key & 15) + lax.rem(ky, 2) * 16
        limit = jnp.where(low, valid_ref[b0], valid_ref[b1])
        first = jnp.where(low, mask_ref[0, b0], mask_ref[0, b1])
        second = jnp.where(low, mask_ref[1, b0], mask_ref[1, b1])
        wanted = jnp.where(col == 0, first, second)
        live = jnp.where(place < limit, wanted, 0)
        live = jnp.where(col < 2, live, 1)
        bias[kx, ky] = jnp.where(live > 0, 0.0, NEG).astype(BF16)
        return carry

    lax.fori_loop(0, NX * NY, mask_block, 0)

    for dz in range(NZ):
        for c in range(2):
            src_z = ring(z + dz, NZ)

            def arrival(cc):
                return pltpu.make_async_remote_copy(
                    src_ref=own.at[0],
                    dst_ref=stage.at[src_z, cc],
                    send_sem=z_send.at[0, 1],
                    recv_sem=z_recv.at[src_z, cc],
                    device_id=sib,
                    device_id_type=MESH,
                )

            if dz == 0:
                if c == 0:
                    arrival(1 - core).wait_recv()
            else:
                arrival(c).wait_recv()
    plain = stage[...].astype(F32).reshape(128, D)
    turned = jnp.concatenate([plain[:, p * 128 : (p + 1) * 128].T for p in range(PAIRS)], axis=1)
    block = jnp.where(core == 0, plain, turned).astype(BF16)

    uv = ((x, y), (y, x))
    for half in range(2):
        u, v = uv[half]
        kv[core, half, u, v] = block[:, half * 256 : (half + 1) * 256]

    def dev_of(half, u, v, c):
        return device(u, v, z, c) if half == 0 else device(v, u, z, c)

    slots = {}

    def copy_block(half, bu, bv, name, target, recv):
        slot = slots.setdefault((half, name), len(slots))
        return pltpu.make_async_remote_copy(
            src_ref=kv.at[core, half, bu, bv],
            dst_ref=kv.at[core, half, bu, bv],
            send_sem=send_sem.at[slot],
            recv_sem=recv.at[half, bu, bv],
            device_id=target,
            device_id_type=MESH,
        )

    sent = []

    def send(half, bu, bv, name, target, recv=None):
        copy = copy_block(half, bu, bv, name, target, near_recv if recv is None else recv)
        copy.start()
        sent.append(copy)

    def wait_near(half, bu, bv):
        pltpu.make_async_remote_copy(
            src_ref=kv.at[core, half, bu, bv],
            dst_ref=kv.at[core, half, bu, bv],
            send_sem=send_sem.at[0],
            recv_sem=near_recv.at[half, bu, bv],
            device_id=sib,
            device_id_type=MESH,
        ).wait_recv()

    def wait_sib(half, bu, bv):
        pltpu.make_async_remote_copy(
            src_ref=kv.at[1 - core, half, bu, bv],
            dst_ref=kv.at[1 - core, half, bu, bv],
            send_sem=send_sem.at[0],
            recv_sem=sib_recv.at[half, bu, bv],
            device_id=sib,
            device_id_type=MESH,
        ).wait_recv()

    def spread(half, bv, tag):
        u, v = uv[half]
        for d in (1, 3):
            send(half, u, bv, ("u", tag, d), dev_of(half, ring(u + d, 4), v, core))
        send(half, u, bv, ("sib", tag), sib, sib_recv)


    def attend(half, blocks, first):
        ones = jnp.ones((16, 128 * len(blocks)), BF16)
        for p in range(2):
            pair = half * 2 + p
            cols = slice(p * 128, (p + 1) * 128)
            keys = [kv[0, half, bu, bv, :, cols] for bu, bv in blocks]
            values = [kv[1, half, bu, bv, :, cols] for bu, bv in blocks]
            shut = [bias[bu, bv] if half == 0 else bias[bv, bu] for bu, bv in blocks]
            scores = jnp.dot(
                jnp.concatenate(
                    [jnp.concatenate(keys, axis=0), jnp.concatenate(shut, axis=0)], axis=1
                ),
                qt[pair],
                preferred_element_type=F32,
            )
            peak = jnp.max(scores, axis=0, keepdims=True)
            if first:
                new_top = jnp.broadcast_to(peak, (8, 512))
            else:
                old_top = top[pair]
                new_top = jnp.maximum(old_top, peak)
            weights = jnp.exp(scores - new_top[:1]).astype(BF16)
            part = jnp.dot(
                jnp.concatenate([jnp.concatenate(values, axis=1), ones], axis=0),
                weights,
                preferred_element_type=F32,
            )
            if first:
                acc[pair] = part
            else:
                factor = jnp.exp(old_top - new_top)
                acc[pair] = acc[pair] * factor[:1] + part
            top[pair] = new_top

    us = []
    vs = []
    for half in range(2):
        u, v = uv[half]
        us.append((u, ring(u - side, 4), ring(u + side, 4), ring(u + 2, 4)))
        vs.append((v, ring(v + 1, 4), ring(v - 1, 4), ring(v + 2, 4)))
    OWN, NEXT, PREV, FAR = 0, 1, 2, 3
    BACK, AHEAD = 1, 2

    def both(step, *args):
        for half in range(2):
            step(half, *args)

    def line_sends(half):
        u, v = uv[half]
        for d in (1, 3):
            send(half, u, v, ("v", d), dev_of(half, u, ring(v + d, 4), core))

    def line_near(half):
        u, v = uv[half]
        wait_near(half, u, vs[half][NEXT])
        spread(half, vs[half][NEXT], NEXT)
        wait_near(half, u, vs[half][PREV])
        spread(half, vs[half][PREV], PREV)

    def line_far(half):
        wait_near(half, uv[half][0], vs[half][FAR])
        spread(half, vs[half][FAR], FAR)

    def from_back(half, c):
        bu, bv = us[half][BACK], vs[half][c]
        wait_near(half, bu, bv)
        send(half, bu, bv, ("relay", c), dev_of(half, us[half][AHEAD], uv[half][1], core))
        send(half, bu, bv, ("sib1", c), sib, sib_recv)

    def from_ahead(half, c):
        bu, bv = us[half][AHEAD], vs[half][c]
        wait_near(half, bu, bv)
        send(half, bu, bv, ("sib2", c), sib, sib_recv)

    def from_far(half, c):
        bu, bv = us[half][FAR], vs[half][c]
        wait_near(half, bu, bv)
        send(half, bu, bv, ("sib3", c), sib, sib_recv)

    def chunk(half, places, first=False):
        blocks = [(us[half][a], vs[half][b]) for a, b in places]
        for bu, bv in blocks:
            wait_sib(half, bu, bv)
        attend(half, blocks, first)

    line = [(OWN, c) for c in (OWN, NEXT, PREV, FAR)]
    close = [(a, c) for a in (BACK, AHEAD) for c in (OWN, NEXT)]
    wide_off = [(a, c) for a in (BACK, AHEAD) for c in (PREV, FAR)]
    early = [(FAR, c) for c in (OWN, NEXT)]
    last = [(FAR, c) for c in (PREV, FAR)]

    both(line_sends)
    for half in range(2):
        spread(half, uv[half][1], OWN)
    for half in range(2):
        u, v = uv[half]
        send(half, u, v, ("v", 2), dev_of(half, u, ring(v + 2, 4), core))
    both(line_near)
    both(from_back, OWN)
    both(from_ahead, OWN)
    both(line_far)
    chunk(0, line, True)
    both(from_back, NEXT)
    both(from_ahead, NEXT)
    chunk(1, line, True)
    both(from_back, PREV)
    both(from_ahead, PREV)
    both(from_far, OWN)
    chunk(0, close)
    both(from_back, FAR)
    both(from_ahead, FAR)
    chunk(1, close)
    both(from_far, NEXT)
    chunk(0, wide_off)
    chunk(1, wide_off)
    both(from_far, PREV)
    both(from_far, FAR)
    chunk(0, early)
    chunk(1, early)
    chunk(0, last)
    chunk(1, last)

    for pair in range(PAIRS):
        share = 1.0 / acc[pair, 128:129, :]
        even = acc[pair, :64, :ROWS] * share[:, :ROWS]
        odd = acc[pair, 64:128, ROWS:] * share[:, ROWS:]
        mixed[:, pair * 128 : (pair + 1) * 128] = jnp.concatenate([even, odd], axis=0).T.astype(BF16)

    loads[3].wait()
    loads[4].wait()
    up = pltpu.make_async_remote_copy(
        src_ref=nrm.at[0], dst_ref=halo.at[1], send_sem=halo_send.at[0],
        recv_sem=halo_recv.at[1], device_id=prv_id, device_id_type=MESH,
    )
    down = pltpu.make_async_remote_copy(
        src_ref=nrm.at[1], dst_ref=halo.at[0], send_sem=halo_send.at[1],
        recv_sem=halo_recv.at[0], device_id=nxt_id, device_id_type=MESH,
    )
    for row_at, copy in ((1, down), (0, up)):
        rows = slice(row_at * LON, (row_at + 1) * LON)
        projected = jnp.dot(mixed[rows], wo[...], preferred_element_type=F32)
        hidden = (feat[rows].astype(F32) + projected).astype(BF16)
        wide = hidden.astype(F32)
        feat[rows] = hidden
        scale = lax.rsqrt(jnp.mean(wide * wide, axis=-1, keepdims=True) + 1e-06)
        nrm[row_at] = (wide * scale).astype(BF16)
        copy.start()

    def neighbours(field):
        wide_field = field.astype(F32)
        left = pltpu.roll(wide_field, 1, 0).astype(BF16)
        right = pltpu.roll(wide_field, LON - 1, 0).astype(BF16)
        return jnp.concatenate([left, field, right], axis=1)

    loads[5].wait()
    pair_rows = jnp.concatenate([neighbours(nrm[0]), neighbours(nrm[1])], axis=1)
    top_row = jnp.dot(pair_rows, wc[1:3].reshape(6 * D, D), preferred_element_type=F32)
    low_row = jnp.dot(pair_rows, wc[0:2].reshape(6 * D, D), preferred_element_type=F32)

    down.wait_recv()
    above = jnp.where(me > 0, halo[0].astype(F32), 0.0).astype(BF16)
    top_row = top_row + jnp.dot(
        neighbours(above), wc[0].reshape(3 * D, D), preferred_element_type=F32
    )
    out_ref[:LON] = (feat[:LON].astype(F32) + top_row).astype(BF16)
    upper = pltpu.make_async_copy(out_ref.at[:LON], out_hbm.at[:LON], out_sem.at[0])
    upper.start()
    up.wait_recv()
    below = jnp.where(me < 255, halo[1].astype(F32), 0.0).astype(BF16)
    low_row = low_row + jnp.dot(
        neighbours(below), wc[2].reshape(3 * D, D), preferred_element_type=F32
    )
    out_ref[LON:] = (feat[LON:].astype(F32) + low_row).astype(BF16)
    lower = pltpu.make_async_copy(out_ref.at[LON:], out_hbm.at[LON:], out_sem.at[1])
    lower.start()

    for dz in range(1, NZ):
        for c in range(2):
            z_copy(dz, c).wait_send()
    sib_copy.wait_send()
    for copy in sent:
        copy.wait_send()
    up.wait_send()
    down.wait_send()
    upper.wait()
    lower.wait()


def on_device(grid_feat, queries, obs_keys, obs_values, block_mask, obs_valid, out_weight, conv_weight):
    hbm = pl.BlockSpec(memory_space=pltpu.HBM)
    return pl.pallas_call(
        kernel,
        out_shape=jax.ShapeDtypeStruct((ROWS, D), BF16),
        in_specs=[hbm] * 8,
        out_specs=hbm,
        scratch_shapes=[
            pltpu.SMEM((2, 16), jnp.int32),
            pltpu.SMEM((16,), jnp.int32),
            pltpu.VMEM((2, 8, D), BF16),
            pltpu.VMEM((NZ, 2, 8, D), BF16),
            pltpu.VMEM((2, 2, 4, 4, 128, 256), BF16),
            pltpu.VMEM((NX, NY, 128, 128), BF16),
            pltpu.VMEM((ROWS, D), BF16),
            pltpu.VMEM((PAIRS, 256, 512), BF16),
            pltpu.VMEM((ROWS, D), BF16),
            pltpu.VMEM((D, D), BF16),
            pltpu.VMEM((3, 3, D, D), BF16),
            pltpu.VMEM((PAIRS, 144, 512), F32),
            pltpu.VMEM((PAIRS, 8, 512), F32),
            pltpu.VMEM((ROWS, D), BF16),
            pltpu.VMEM((2, LON, D), BF16),
            pltpu.VMEM((2, LON, D), BF16),
            pltpu.SemaphoreType.DMA((8,)),
            pltpu.SemaphoreType.DMA((NZ, 2)),
            pltpu.SemaphoreType.DMA((NZ, 2)),
            pltpu.SemaphoreType.DMA((64,)),
            pltpu.SemaphoreType.DMA((2, 4, 4)),
            pltpu.SemaphoreType.DMA((2, 4, 4)),
            pltpu.SemaphoreType.DMA((2,)),
            pltpu.SemaphoreType.DMA((2,)),
            pltpu.VMEM((ROWS, D), BF16),
            pltpu.SemaphoreType.DMA((2,)),
        ],
        compiler_params=pltpu.CompilerParams(
            collective_id=0, has_side_effects=True, vmem_limit_bytes=58 * 1024 * 1024
        ),
    )(block_mask, obs_valid, grid_feat, queries, obs_keys, obs_values, out_weight, conv_weight)


def solution(mesh):
    rows = P(("blk", "tile"), None)
    return jax.shard_map(
        on_device,
        mesh=mesh,
        in_specs=(rows, rows, rows, rows, rows, P(), P(), P()),
        out_specs=rows,
        check_vma=False,
    )
```
